256 devices in a mesh: pert: 8 (over z_lo, y), space: 32 (over x, z_hi, core).
Axes of the slice: x: 4, y: 4, z: 8 (z_hi: 4, z_lo: 2; z = z_hi * 2 + z_lo), core: 2. Of those that a mesh axis runs over, the one named last changes fastest.
Arguments:
- spectra: float32 [320, 320, 1024], P('space', None, 'pert'), may hold values from -6 to 6
- wave_order: int32 [320], replicated, may hold values from 0 to 319, as said below
- traj_wind: bfloat16 [2, 32, 480, 960], P(None, 'pert', 'space'), may hold values from -0.029907227 to 0.029907227
- traj_state: bfloat16 [2, 2, 32, 480, 960], P(None, None, 'pert', 'space'), may hold values from -6 to 6
- vertical_modes: float32 [32, 32], replicated, may hold values from -0.75 to 0.75
- mode_speeds: float32 [32], replicated, may hold values from 1e-06 to 0.001
Outputs:
- spectra_out: float32 [320, 320, 1024], P('space', None, 'pert')
The draws below stay inside these ranges and needn't reach their ends.
Inputs may be any that keep to these rules, and one draw needn't show every extreme that they name: wave_order is a permutation of 0 to 319 in which slots 2 i and 2 i + 1 hold two wavenumbers that add up to 319.
All inputs are finite; a program needn't handle non-finite values.
Results may differ from the reference program's by a relative error of at most 0.0085.
Values may be sent and summed in bfloat16 or wider, within the bound.
A program may use at most 128 MiB of HBM per device.

```python
import math
import jax
import jax.numpy as jnp
from jax import lax

NLAT = 480
NLON = 960
M = 320
VARS = 2
LEV = 32
STEPS = 2
CH = 1024


def draw_wave_order(key, part):
    pair_count = M // 2
    key_pairs = jax.random.fold_in(key, 11)
    key_flips = jax.random.fold_in(key, 12)
    pair_order = jax.random.permutation(key_pairs, pair_count).astype(jnp.int32)
    flip_bits = jax.random.randint(key_flips, (pair_count,), 0, 2).astype(jnp.int32)
    lower_wave = pair_order
    upper_wave = M - 1 - pair_order
    leading = jnp.where(flip_bits == 1, upper_wave, lower_wave)
    trailing = jnp.where(flip_bits == 1, lower_wave, upper_wave)
    return jnp.stack([leading, trailing], axis=1).reshape(M).astype(jnp.int32)


def block_scale(stream_key, shape, pieces, smallest, top_value):
    gain, own = 1.0, jax.random.fold_in(stream_key, 6)
    for position, parts in pieces:
        draws = jnp.exp(jax.random.uniform(jax.random.fold_in(own, position), (parts,), jnp.float32, smallest / len(pieces), top_value / len(pieces)))
        gain = gain * jnp.repeat(draws, shape[position] // parts).reshape([-1 if axis == position else 1 for axis in range(len(shape))])
    return gain


def gaussian(rng, shape, deviation, most, pieces=(), kind=jnp.bfloat16):
    array = jax.random.normal(rng, shape, jnp.float32) * deviation
    if len(pieces) > 0:
        array = block_scale(rng, shape, pieces, -0.22, 0.18) * array
    return jnp.clip(array, min=-most, max=most).astype(kind)


def setup_inputs(seed: int = 0) -> dict:
    seeds = jax.random.split(jax.random.key(seed), 7)
    spectra = gaussian(seeds[0], (M, M, CH), 1.0, 6.0, ((0, 32), (2, 8)), jnp.float32)
    wave_order = draw_wave_order(jax.random.fold_in(seeds[6], 71), 0)
    traj_wind = gaussian(seeds[2], (STEPS, LEV, NLAT, NLON), 0.005, 0.029907227, ((1, 8), (2, 32)))
    traj_state = gaussian(seeds[3], (STEPS, VARS, LEV, NLAT, NLON), 1.0, 6.0, ((2, 8), (3, 32)))
    vertical_modes = gaussian(seeds[4], (LEV, LEV), (2 * LEV) ** -0.5, 0.75, (), jnp.float32)
    mode_speeds = jnp.clip(jnp.exp(jax.random.uniform(seeds[5], (LEV,), jnp.float32, math.log(9.999999974752427e-07), math.log(0.001))), 9.999999974752427e-07, 0.001)
    return {"spectra": spectra, "wave_order": wave_order, "traj_wind": traj_wind, "traj_state": traj_state, "vertical_modes": vertical_modes, "mode_speeds": mode_speeds}


def grid_angles():
    colatitude = (jnp.arange(NLAT, dtype=jnp.float32) + 0.5) * (math.pi / NLAT)
    return (jnp.cos(colatitude), jnp.sin(colatitude))

def sectoral_log(wave_float, sine_values):
    gammas = jax.scipy.special.gammaln
    start = 0.5 * (gammas(wave_float + 1.5) - gammas(wave_float + 1.0) - gammas(jnp.float32(1.5))) - 0.5 * math.log(2.0)
    return start[:, None] + wave_float[:, None] * jnp.log(sine_values)[None, :]

def coefficient(wave_float, degree):
    return jnp.sqrt((4.0 * degree * degree - 1.0) / ((degree - wave_float) * (degree + wave_float)))

def legendre_table(wave_list):
    cosines, sine_values = grid_angles()
    wave_float = wave_list.astype(jnp.float32)[:, None]
    log_start = sectoral_log(wave_list.astype(jnp.float32), sine_values)
    second = jnp.sqrt(2.0 * wave_float + 3.0) * cosines[None, :]
    largest = jnp.maximum(jnp.abs(second), 1.0)
    initial = (second / largest, 1.0 / largest, jnp.log(largest))
    row_zero = jnp.exp(log_start)
    row_one = second / largest * jnp.exp(log_start + jnp.log(largest))

    def advance(loop_carry, offset):
        current, previous, log_scale = loop_carry
        degree = wave_float + offset.astype(jnp.float32)
        upper_coef = coefficient(wave_float, degree)
        lower_coef = coefficient(wave_float, degree - 1.0)
        following = upper_coef * (cosines[None, :] * current - previous / lower_coef)
        biggest = jnp.maximum(jnp.abs(following), jnp.abs(current))
        log_next = log_scale + jnp.log(biggest)
        scaled = following / biggest
        return ((scaled, current / biggest, log_next), scaled * jnp.exp(log_start + log_next))
    offsets = jnp.arange(2, M, dtype=jnp.int32)
    final_carry, later_rows = lax.scan(advance, initial, offsets)
    stacked = jnp.concatenate([row_zero[None], row_one[None], later_rows], axis=0)
    legendre = jnp.moveaxis(stacked, 0, 1)
    inside = wave_list[:, None] + jnp.arange(M, dtype=jnp.int32)[None, :] <= M - 1
    return legendre * inside[:, :, None].astype(jnp.float32)

def zonal_tables(wave_list):
    cell_index = jnp.arange(NLON, dtype=jnp.int32)
    phase_index = wave_list[:, None] * cell_index[None, :] % NLON
    angles = phase_index.astype(jnp.float32) * (2.0 * math.pi / NLON)
    factor = jnp.where(wave_list == 0, 1.0, 2.0).astype(jnp.float32)[:, None]
    synth_table = jnp.stack([factor * jnp.cos(angles), -factor * jnp.sin(angles)]).astype(jnp.bfloat16)
    analysis = (jnp.stack([jnp.cos(angles).T, -jnp.sin(angles).T], axis=1) / NLON).astype(jnp.bfloat16)
    return (synth_table, analysis)

def spectral_mask(wave_list, columns):
    degree_offset = jnp.arange(M, dtype=jnp.int32)
    inside = wave_list[:, None] + degree_offset[None, :] <= M - 1
    imaginary = jnp.arange(columns, dtype=jnp.int32) % 2 == 1
    dropped = (wave_list[:, None] == 0) & imaginary[None, :]
    return (inside[:, :, None] & jnp.logical_not(dropped)[:, None, :]).astype(jnp.float32)

def damping_rates(wave_list, mode_speeds):
    degree = (wave_list[:, None] + jnp.arange(M, dtype=jnp.int32)[None, :]).astype(jnp.float32)
    stiffness = mode_speeds[None, None, :] * (degree * (degree + 1.0))[:, :, None]
    return stiffness / (1.0 + stiffness)

def zonal_slope(fourier, wave_list):
    part_pairs = fourier.reshape(fourier.shape[:-1] + (fourier.shape[-1] // 2, 2)).astype(jnp.float32)
    factor = wave_list.astype(jnp.float32).reshape((-1,) + (1,) * (part_pairs.ndim - 1))
    turned = jnp.stack([-part_pairs[..., 1], part_pairs[..., 0]], axis=-1) * factor
    return turned.reshape(fourier.shape).astype(jnp.bfloat16)

def synthesis(fourier, synth_table):
    part_pairs = fourier.reshape(fourier.shape[0], fourier.shape[1], -1, 2).astype(jnp.float32)
    return jnp.einsum('jtrc,cjx->trx', part_pairs, synth_table.astype(jnp.float32))

def tendency(grid_values, grid_slopes, wind_now, traj_now):
    lat_count = grid_values.shape[0]
    shaped = (lat_count, -1, VARS, LEV, NLON)
    values_five = grid_values.reshape(shaped)
    slopes_five = grid_slopes.reshape(shaped)
    wind_rows = jnp.transpose(wind_now, (1, 0, 2)).astype(jnp.float32)[:, None, None, :, :]
    state_rows = jnp.roll(jnp.transpose(traj_now, (2, 0, 1, 3)), -1, axis=1).astype(jnp.float32)[:, None]
    shifted = jnp.roll(values_five, -2, axis=2)
    forcing = -wind_rows * slopes_five - state_rows * shifted
    return forcing.reshape(lat_count, -1, NLON).astype(jnp.bfloat16)

def analysis_step(forcing, analysis):
    lat_count = forcing.shape[0]
    fourier = jnp.einsum('trx,xcj->jtrc', forcing.astype(jnp.float32), analysis.astype(jnp.float32))
    return fourier.astype(jnp.bfloat16).reshape(analysis.shape[2], lat_count, -1)

def reference(spectra, wave_order, traj_wind, traj_state, vertical_modes, mode_speeds):
    legendre = legendre_table(wave_order)
    angle_pair = grid_angles()
    inverse_table = legendre.astype(jnp.bfloat16)
    forward_table = (legendre * (angle_pair[1] * (math.pi / NLAT))[None, None, :]).astype(jnp.bfloat16)
    synth_table, analysis = zonal_tables(wave_order)
    member_cols = 2 * VARS * LEV
    members = jnp.moveaxis(spectra.reshape(M, M, -1, member_cols), 2, 0)
    keep_mask = spectral_mask(wave_order, member_cols)
    damping = damping_rates(wave_order, mode_speeds)

    def advance_member(member):
        spectral_state = member * keep_mask
        for step_idx in range(STEPS):
            fourier_rows = jnp.einsum('jkt,jkc->jtc', inverse_table.astype(jnp.float32), spectral_state.astype(jnp.bfloat16).astype(jnp.float32)).astype(jnp.bfloat16)
            slope_rows = zonal_slope(fourier_rows, wave_order)
            grid_values = synthesis(fourier_rows, synth_table)
            grid_slopes = synthesis(slope_rows, synth_table)
            forcing = tendency(grid_values, grid_slopes, traj_wind[step_idx], traj_state[step_idx])
            wave_rows = analysis_step(forcing, analysis)
            change = jnp.einsum('jkt,jtc->jkc', forward_table.astype(jnp.float32), wave_rows.astype(jnp.float32))
            combined = spectral_state + change
            shaped = combined.reshape(M, M, VARS, LEV, 2)
            projected = jnp.einsum('ab,jkvbc->jkvac', vertical_modes, shaped, precision=lax.Precision.HIGHEST)
            weighted = projected * damping[:, :, None, :, None]
            returned = jnp.einsum('ab,jkvac->jkvbc', vertical_modes, weighted, precision=lax.Precision.HIGHEST)
            spectral_state = (combined - returned.reshape(combined.shape)) * keep_mask
        return spectral_state
    result = lax.map(advance_member, members)
    return jnp.moveaxis(result, 0, 2).reshape(M, M, -1)
```

```python
import math

import jax
import jax.numpy as jnp
import numpy as np
from jax import lax
from jax.experimental import pallas as pl
from jax.experimental.pallas import tpu as pltpu
from jax.sharding import PartitionSpec as P

NLAT = 480
NLON = 960
M = 320
VARS = 2
LEV = 32
STEPS = 2
SPACE = 32
SLOTS = M // SPACE
LATS = NLAT // SPACE
PAD = 16
HALF = (SPACE // 2) * PAD
COLS = 128
ROWS = COLS // 2
HK = M // 2
CHUNKS = 8
GROUP = 4
F32 = jnp.float32
BF16 = jnp.bfloat16
MESH = pl.DeviceIdType.MESH
HIGHEST = lax.Precision.HIGHEST


def dot(a, b, dims=((1,), (0,)), precision=None):
    return lax.dot_general(
        a, b, (dims, ((), ())), preferred_element_type=F32, precision=precision
    )


def iota(shape, axis):
    return lax.broadcasted_iota(jnp.int32, shape, axis)


def reordered(old, new):
    part, row = new // ROWS, new % ROWS
    level = row // 8 * 4 + row % 4
    variable = row % 8 // 4
    return old == variable * 64 + level * 2 + part


def northern():
    place = np.arange(HALF)
    inside = place % PAD < LATS
    lat = np.minimum(place // PAD * LATS + place % PAD, NLAT // 2 - 1)
    angle = (lat + 0.5) * (math.pi / NLAT)
    weight = np.where(inside, np.sin(angle) * (math.pi / NLAT), 0.0)
    rows = np.stack([np.cos(angle), np.log(np.sin(angle)), inside.astype(np.float64)])
    return rows.astype(np.float32), np.repeat(weight[:, None], COLS, 1).astype(np.float32)


def table_kernel(
    wave_smem, wave_ref, lat_ref, spectra_ref, modes_ref, speeds_ref,
    table_ref, state_ref, send_ref, mix_ref, speed_ref, scratch,
):
    lev = iota((LEV, COLS), 0)
    column = iota((LEV, COLS), 1)
    onehot = (column // 2 % LEV == lev).astype(F32)
    spread = dot(onehot, modes_ref[...], ((0,), (1,)), HIGHEST)
    group = lambda c: c // (2 * LEV) * 2 + c % 2
    same = group(iota((COLS, COLS), 0)) == group(iota((COLS, COLS), 1))
    mix_ref[...] = dot(spread, onehot, precision=HIGHEST) * same.astype(F32)
    speed_ref[...] = dot(speeds_ref[...], onehot, precision=HIGHEST)

    wave = wave_ref[...]
    cosines = [lat_ref[0:1, c * 128 : (c + 1) * 128] for c in range(2)]
    number = (iota((16, 384), 1) + 1).astype(F32)
    terms = jnp.where(number <= wave[:, 0:1], jnp.log((2.0 * number + 1.0) / (2.0 * number)), 0.0)
    start = 0.5 * jnp.sum(terms, axis=1, keepdims=True) - 0.5 * math.log(2.0)
    starts = [
        start + wave * lat_ref[1:2, c * 128 : (c + 1) * 128] for c in range(2)
    ]
    inside = [lat_ref[2:3, c * 128 : (c + 1) * 128] for c in range(2)]

    def block(b, carry):
        current, previous, logs, last = carry
        current, previous, logs = list(current), list(previous), list(logs)
        factor = [jnp.exp(starts[c] + logs[c]) * inside[c] for c in range(2)]
        first = b * 16
        for i in range(16):
            k = (first + i).astype(F32)
            keep = (wave + k <= M - 1.0).astype(F32)
            row = (i % 2) * HK + b * 8 + i // 2
            for c in range(2):
                scratch[c, pl.ds(row, 16, stride=M), :] = current[c] * (factor[c] * keep)
            up = k + 1.0
            degree2 = 2.0 * (wave + up)
            coef = jnp.sqrt((degree2 * degree2 - 1.0) / (up * (2.0 * wave + up)))
            ratio = coef / last
            for c in range(2):
                following = coef * cosines[c] * current[c] - ratio * previous[c]
                previous[c] = current[c]
                current[c] = following
            last = coef
        for c in range(2):
            biggest = jnp.maximum(jnp.abs(current[c]), jnp.abs(previous[c]))
            shrink = 1.0 / biggest
            current[c] = current[c] * shrink
            previous[c] = previous[c] * shrink
            logs[c] = logs[c] + jnp.log(biggest)
        return tuple(current), tuple(previous), tuple(logs), last

    ones = jnp.ones((16, 128), F32)
    zeros = jnp.zeros((16, 128), F32)
    lax.fori_loop(0, M // 16, block, ((ones, ones), (zeros, zeros), (zeros, zeros), ones))

    perm = reordered(iota((COLS, COLS), 0), iota((COLS, COLS), 1)).astype(BF16)
    imaginary = iota((HK, COLS), 1) % 2 == 1
    half_degree = 2 * iota((HK, COLS), 0)

    def slot(j, _):
        w = wave_smem[j]
        for parity in range(2):
            for c in range(2):
                table_ref[j, parity, :, c * 128 : (c + 1) * 128] = scratch[
                    c, pl.ds(j * M + parity * HK, HK), :
                ].astype(BF16)
            keep = (half_degree + (parity + w) <= M - 1) & jnp.logical_not(imaginary & (w == 0))
            state_ref[j, parity] = spectra_ref[j, pl.ds(parity, HK, stride=2), :] * keep.astype(F32)
        legendre_rows(j, table_ref, state_ref[j, 0], state_ref[j, 1], perm, send_ref)
        return 0

    lax.fori_loop(0, SLOTS, slot, 0)


def legendre_rows(j, table_ref, even_state, odd_state, perm, send_ref):
    even = dot(
        table_ref[j, 0], dot(even_state.astype(BF16), perm).astype(BF16), ((0,), (0,))
    )
    odd = dot(
        table_ref[j, 1], dot(odd_state.astype(BF16), perm).astype(BF16), ((0,), (0,))
    )
    north = (even + odd).astype(BF16)
    south = (even - odd).astype(BF16)
    for d in range(SPACE // 2):
        send_ref[d, j] = north[d * PAD : (d + 1) * PAD]
        send_ref[SPACE - 1 - d, j] = south[d * PAD : (d + 1) * PAD]


def update_kernel(last, wave_smem, weight_ref, table_ref, state_ref, rows_ref, mix_ref, speed_ref, *outs):
    perm = reordered(iota((COLS, COLS), 1), iota((COLS, COLS), 0)).astype(BF16)
    perm_forward = reordered(iota((COLS, COLS), 0), iota((COLS, COLS), 1)).astype(BF16)
    imaginary = iota((HK, COLS), 1) % 2 == 1
    half_degree = 2 * iota((HK, COLS), 0)
    weight = weight_ref[...]
    speed = speed_ref[0:1, :]

    def slot(j, _):
        w = wave_smem[j]
        north = jnp.concatenate([rows_ref[d, j] for d in range(SPACE // 2)], axis=0).astype(F32)
        south = jnp.concatenate(
            [rows_ref[SPACE - 1 - d, j] for d in range(SPACE // 2)], axis=0
        ).astype(F32)
        new = []
        for parity in range(2):
            both = (north + south if parity == 0 else north - south) * weight
            columns = dot(both.astype(BF16), perm).astype(BF16)
            change = dot(table_ref[j, parity], columns)
            combined = state_ref[j, parity] + change
            degree = half_degree + (parity + w)
            keep = (degree <= M - 1) & jnp.logical_not(imaginary & (w == 0))
            stiffness = speed * (degree * (degree + 1)).astype(F32)
            damping = stiffness / (1.0 + stiffness)
            projected = dot(combined, mix_ref[...], precision=HIGHEST)
            returned = dot(damping * projected, mix_ref[...], ((1,), (1,)), HIGHEST)
            new.append((combined - returned) * keep.astype(F32))
        if last:
            for parity in range(2):
                outs[0][j, pl.ds(parity, HK, stride=2), :] = new[parity]
        else:
            for parity in range(2):
                outs[0][j, parity] = new[parity]
            legendre_rows(j, table_ref, new[0], new[1], perm_forward, outs[1])
        return 0

    lax.fori_loop(0, SLOTS, slot, 0)


def zonal_kernel(wave_ref, synth_ref, analysis_ref):
    wave = wave_ref[...]
    step = 2.0 * math.pi / NLON

    def angle_of(count):
        return (count - NLON * jnp.floor(count * (1.0 / NLON))) * step

    x = iota((M, 128), 1).astype(F32)
    angle = angle_of(wave * x)
    turn = angle_of(wave * jnp.full((M, 128), 128.0, F32))
    cosine, sine = jnp.cos(angle), jnp.sin(angle)
    turn_cosine, turn_sine = jnp.cos(turn), jnp.sin(turn)
    factor = jnp.where(wave == 0.0, 1.0, 2.0)
    for c in range(CHUNKS):
        width = min(128, NLON - c * 128)
        lanes = slice(c * 128, c * 128 + width)
        synth_ref[0:M, lanes] = (factor * cosine)[:, :width].astype(BF16)
        synth_ref[M : 2 * M, lanes] = (-factor * sine)[:, :width].astype(BF16)
        analysis_ref[0:M, lanes] = (cosine * (1.0 / NLON))[:, :width].astype(BF16)
        analysis_ref[M : 2 * M, lanes] = (sine * (-1.0 / NLON))[:, :width].astype(BF16)
        cosine, sine = (
            cosine * turn_cosine - sine * turn_sine,
            sine * turn_cosine + cosine * turn_sine,
        )


def grid_kernel(flip_smem, wave_ref, rows_ref, synth_ref, analysis_ref, traj_ref, out_ref, wide, narrow):
    g = pl.program_id(0)

    @pl.when(g == 0)
    def _():
        def widen(i, _):
            at = pl.ds(pl.multiple_of(i * 512, 512), 512)
            wide[at, :] = rows_ref[at, :].astype(F32)
            return 0

        lax.fori_loop(0, M * PAD // 512, widen, 0)

    wave = wave_ref[...]
    low = iota((M, COLS), 1) < ROWS
    values_in, slopes_in = [], []
    for pair in range(GROUP // 2):
        t = g * GROUP + 2 * pair
        one = wide[pl.ds(t, M, stride=PAD), :]
        two = wide[pl.ds(t + 1, M, stride=PAD), :]
        real = jnp.where(low, one, pltpu.roll(two, ROWS, 1))
        imag = jnp.where(low, pltpu.roll(one, ROWS, 1), two)
        values_in.append(jnp.concatenate([real, imag], axis=0).astype(BF16))
        slopes_in.append(jnp.concatenate([-wave * imag, wave * real], axis=0).astype(BF16))
    values = dot(jnp.concatenate(values_in, axis=1), synth_ref[...], ((0,), (0,)))
    slopes = dot(jnp.concatenate(slopes_in, axis=1), synth_ref[...], ((0,), (0,)))
    pieces = []
    for q in range(GROUP):
        i = jnp.minimum(g * GROUP + q, LATS - 1)
        t = jnp.where(flip_smem[0] == 1, LATS - 1 - i, i)
        now = traj_ref[:, t].astype(F32)
        wind = jnp.concatenate([now[:, 0], now[:, 0]], axis=1)
        state = jnp.concatenate([now[:, 2], now[:, 1]], axis=1)
        v = values[q * ROWS : (q + 1) * ROWS].reshape(8, 8, NLON)
        s = slopes[q * ROWS : (q + 1) * ROWS].reshape(8, 8, NLON)
        pieces.append((-wind * s - state * v).reshape(ROWS, NLON).astype(BF16))
    forcing = jnp.concatenate(pieces, axis=0)
    waves = dot(analysis_ref[...], forcing, ((1,), (1,)))
    for pair in range(GROUP // 2):
        t = g * GROUP + 2 * pair
        real = waves[0:M, pair * COLS : (pair + 1) * COLS]
        imag = waves[M : 2 * M, pair * COLS : (pair + 1) * COLS]
        narrow[pl.ds(t, M, stride=PAD), :] = jnp.where(low, real, pltpu.roll(imag, ROWS, 1))
        narrow[pl.ds(t + 1, M, stride=PAD), :] = jnp.where(low, pltpu.roll(real, ROWS, 1), imag)

    @pl.when(g == PAD // GROUP - 1)
    def _():
        def shrink(i, _):
            at = pl.ds(pl.multiple_of(i * 512, 512), 512)
            out_ref[at, :] = narrow[at, :].astype(BF16)
            return 0

        lax.fori_loop(0, M * PAD // 512, shrink, 0)


def exchange_kernel(src, dst, send_sem, recv_sem, own_sem):
    me = lax.axis_index("space")
    barrier = pltpu.get_barrier_semaphore()

    def greet(i, _):
        pl.semaphore_signal(
            barrier, inc=1, device_id={"space": lax.rem(me + i, SPACE)}, device_id_type=MESH
        )
        return 0

    lax.fori_loop(1, SPACE, greet, 0)
    pl.semaphore_wait(barrier, SPACE - 1)
    own = pltpu.make_async_copy(src.at[me], dst.at[me], own_sem)
    own.start()

    def copy(i):
        to = lax.rem(me + i, SPACE)
        return pltpu.make_async_remote_copy(
            src.at[to], dst.at[me], send_sem.at[i], recv_sem.at[i],
            device_id={"space": to}, device_id_type=MESH,
        )

    def start(i, _):
        copy(i).start()
        return 0

    lax.fori_loop(1, SPACE, start, 0)
    own.wait()

    def finish(i, _):
        origin = lax.rem(me - i + SPACE, SPACE)
        pltpu.make_async_remote_copy(
            src.at[origin], dst.at[origin], send_sem.at[i], recv_sem.at[i],
            device_id={"space": origin}, device_id_type=MESH,
        ).wait_recv()
        copy(i).wait_send()
        return 0

    lax.fori_loop(1, SPACE, finish, 0)


VMEM = pl.BlockSpec(memory_space=pltpu.VMEM)
SMEM = pl.BlockSpec(memory_space=pltpu.SMEM)
PARAMS = pltpu.CompilerParams(vmem_limit_bytes=56 * 2**20)


def exchange(x):
    return pl.pallas_call(
        exchange_kernel,
        out_shape=jax.ShapeDtypeStruct(x.shape, x.dtype),
        in_specs=[pl.BlockSpec(memory_space=pl.ANY)],
        out_specs=pl.BlockSpec(memory_space=pl.ANY),
        scratch_shapes=[
            pltpu.SemaphoreType.DMA((SPACE,)),
            pltpu.SemaphoreType.DMA((SPACE,)),
            pltpu.SemaphoreType.DMA,
        ],
        compiler_params=pltpu.CompilerParams(collective_id=1, has_side_effects=True),
        name="exchange",
    )(x)


def grid_stage(flip, wave_rows, rows, synth, analysis, traj):
    whole = lambda shape: pl.BlockSpec(shape, lambda g: (0,) * len(shape), pipeline_mode=pl.Buffered(1))
    return pl.pallas_call(
        grid_kernel,
        grid=(PAD // GROUP,),
        out_shape=jax.ShapeDtypeStruct((M * PAD, COLS), BF16),
        in_specs=[
            SMEM,
            whole((M, 1)),
            whole((M * PAD, COLS)),
            whole((2 * M, NLON)),
            whole((2 * M, NLON)),
            whole((8, LATS, 3, 4, NLON)),
        ],
        out_specs=pl.BlockSpec((M * PAD, COLS), lambda g: (0, 0), pipeline_mode=pl.Buffered(1)),
        scratch_shapes=[pltpu.VMEM((M * PAD, COLS), F32), pltpu.VMEM((M * PAD, COLS), F32)],
        compiler_params=PARAMS,
        name="grid_stage",
    )(flip, wave_rows, rows, synth, analysis, traj)


def shards(spectra, wave_order, traj_wind, traj_state, vertical_modes, mode_speeds):
    space = lax.axis_index("space")
    lat_rows, weight = northern()
    gathered = []
    for step in range(STEPS):
        fields = jnp.concatenate([traj_wind[step][None], traj_state[step]], axis=0)
        fields = jnp.transpose(fields, (2, 0, 1, 3))
        gathered.append(lax.all_gather(fields, "pert", axis=0))
    wave_here = lax.dynamic_slice_in_dim(wave_order, space * SLOTS, SLOTS)
    wave_wide = jnp.broadcast_to(
        jnp.pad(wave_here, (0, 16 - SLOTS)).astype(F32)[:, None], (16, 128)
    )
    wave_rows = wave_order.astype(F32)[:, None]
    flip = (space >= SPACE // 2).astype(jnp.int32)[None]
    speeds = jnp.broadcast_to(mode_speeds[None], (8, LEV))

    send_shape = jax.ShapeDtypeStruct((SPACE, SLOTS, PAD, COLS), BF16)
    state_shape = jax.ShapeDtypeStruct((SLOTS, 2, HK, COLS), F32)
    table, state, send, mix, speed = pl.pallas_call(
        table_kernel,
        out_shape=(
            jax.ShapeDtypeStruct((SLOTS, 2, HK, HALF), BF16),
            state_shape,
            send_shape,
            jax.ShapeDtypeStruct((COLS, COLS), F32),
            jax.ShapeDtypeStruct((8, COLS), F32),
        ),
        in_specs=[SMEM] + [VMEM] * 5,
        out_specs=(VMEM,) * 5,
        scratch_shapes=[pltpu.VMEM((2, 16 * M, 128), F32)],
        compiler_params=PARAMS,
        name="table_stage",
    )(wave_here, wave_wide, jnp.asarray(lat_rows), spectra, vertical_modes, speeds)
    synth, analysis = pl.pallas_call(
        zonal_kernel,
        out_shape=(jax.ShapeDtypeStruct((2 * M, NLON), BF16),) * 2,
        in_specs=[VMEM],
        out_specs=(VMEM,) * 2,
        compiler_params=PARAMS,
        name="zonal_stage",
    )(wave_rows)

    for step in range(STEPS):
        rows = exchange(send).reshape(M * PAD, COLS)
        waves = grid_stage(flip, wave_rows, rows, synth, analysis, gathered[step])
        back = exchange(waves.reshape(SPACE, SLOTS, PAD, COLS))
        last = step == STEPS - 1
        result = pl.pallas_call(
            lambda *refs, last=last: update_kernel(last, *refs),
            out_shape=jax.ShapeDtypeStruct((SLOTS, M, COLS), F32) if last else (state_shape, send_shape),
            in_specs=[SMEM] + [VMEM] * 6,
            out_specs=VMEM if last else (VMEM, VMEM),
            compiler_params=PARAMS,
            name="last_update" if last else "update",
        )(wave_here, jnp.asarray(weight), table, state, back, mix, speed)
        if last:
            return result
        state, send = result


def solution(mesh):
    placed = (
        P("space", None, "pert"),
        P(),
        P(None, "pert", "space", None),
        P(None, None, "pert", "space", None),
        P(),
        P(),
    )
    return jax.shard_map(
        shards, mesh=mesh, in_specs=placed, out_specs=P("space", None, "pert"), check_vma=False
    )
```

```python
import math

import jax
import jax.numpy as jnp
import numpy as np
from jax import lax
from jax.experimental import pallas as pl
from jax.experimental.pallas import tpu as pltpu
from jax.sharding import PartitionSpec as P

NLAT = 480
NLON = 960
M = 320
VARS = 2
LEV = 32
STEPS = 2
PERT = 8
SPACE = 32
SLOTS = M // SPACE
LATS = NLAT // SPACE
PAD = 16
HALF = (SPACE // 2) * PAD
COLS = 128
ROWS = COLS // 2
HK = M // 2
CHUNKS = 8
GROUP = 4
F32 = jnp.float32
BF16 = jnp.bfloat16
MESH = pl.DeviceIdType.MESH
HIGHEST = lax.Precision.HIGHEST


def dot(a, b, dims=((1,), (0,)), precision=None):
    return lax.dot_general(
        a, b, (dims, ((), ())), preferred_element_type=F32, precision=precision
    )


def iota(shape, axis):
    return lax.broadcasted_iota(jnp.int32, shape, axis)


def level_of(new):
    return new % ROWS // 8 * 4 + new % 4


def group_of(new):
    return new // ROWS * 2 + new % 8 // 4


def reordered(old, new):
    return old == new % 8 // 4 * 64 + level_of(new) * 2 + new // ROWS


def split(x):
    high = x.astype(BF16)
    return jnp.concatenate([high, (x - high.astype(F32)).astype(BF16)], axis=1)


def northern():
    place = np.arange(HALF)
    inside = place % PAD < LATS
    lat = np.minimum(place // PAD * LATS + place % PAD, NLAT // 2 - 1)
    angle = (lat + 0.5) * (math.pi / NLAT)
    rows = np.stack([np.cos(angle), np.log(np.sin(angle)), inside.astype(np.float64)])
    weight = np.sin((np.arange(NLAT // 2) + 0.5) * (math.pi / NLAT)) * (math.pi / NLAT)
    return rows.astype(np.float32), weight.astype(np.float32)


def keep_of(w):
    row = iota((M, COLS), 0)
    degree = jnp.where(row < HK, 2 * row, 2 * row - (M - 1)) + w
    keep = (degree <= M - 1) & jnp.logical_not((iota((M, COLS), 1) >= ROWS) & (w == 0))
    return keep.astype(F32), degree


def legendre_rows(j, table_ref, state, send_ref):
    even, odd = state[:HK], state[HK:]
    both = jnp.concatenate(
        [jnp.concatenate([even, even], axis=1), jnp.concatenate([odd, -odd], axis=1)], axis=0
    )
    rows = dot(table_ref[j], both, ((0,), (0,))).astype(BF16)
    for d in range(SPACE // 2):
        send_ref[d, j] = rows[d * PAD : (d + 1) * PAD, :COLS]
        send_ref[SPACE - 1 - d, j] = rows[d * PAD : (d + 1) * PAD, COLS:]


def table_kernel(
    wave_smem, lat_ref, spectra_ref, modes_ref, speeds_ref,
    table_ref, state_ref, send_ref, mix_ref, speed_ref, scratch,
):
    lev = iota((LEV, COLS), 0)
    onehot = (level_of(iota((LEV, COLS), 1)) == lev).astype(F32)
    same = (group_of(iota((COLS, COLS), 0)) == group_of(iota((COLS, COLS), 1))).astype(F32)
    for way in range(2):
        spread = dot(onehot, modes_ref[...], ((0,), (1 - way,)), HIGHEST)
        mix = dot(spread, onehot, precision=HIGHEST) * same
        high = mix.astype(BF16)
        low = (mix - high.astype(F32)).astype(BF16)
        mix_ref[way, :COLS, :COLS] = high
        mix_ref[way, :COLS, COLS:] = low
        mix_ref[way, COLS:, :COLS] = high
        mix_ref[way, COLS:, COLS:] = jnp.zeros_like(low)
    speed_ref[...] = dot(jnp.broadcast_to(speeds_ref[...], (8, LEV)), onehot, precision=HIGHEST)

    base = lax.axis_index("space") * SLOTS
    row16 = iota((16, 128), 0)
    wave = jnp.zeros((16, 128), jnp.int32)
    for j in range(SLOTS):
        wave = jnp.where(row16 == j, wave_smem[base + j], wave)
    wave = wave.astype(F32)
    cosines = [lat_ref[0:1, c * 128 : (c + 1) * 128] for c in range(2)]
    number = (iota((16, 384), 1) + 1).astype(F32)
    terms = jnp.where(number <= wave[:, 0:1], jnp.log((2.0 * number + 1.0) / (2.0 * number)), 0.0)
    start = 0.5 * jnp.sum(terms, axis=1, keepdims=True) - 0.5 * math.log(2.0)
    starts = [start + wave * lat_ref[1:2, c * 128 : (c + 1) * 128] for c in range(2)]
    inside = [lat_ref[2:3, c * 128 : (c + 1) * 128] for c in range(2)]

    def block(b, carry):
        current, previous, logs, last = carry
        current, previous, logs = list(current), list(previous), list(logs)
        factor = [jnp.exp(starts[c] + logs[c]) * inside[c] for c in range(2)]
        first = b * 16
        for i in range(16):
            k = (first + i).astype(F32)
            keep = (wave + k <= M - 1.0).astype(F32)
            row = (i % 2) * HK + b * 8 + i // 2
            for c in range(2):
                scratch[c, pl.ds(row, 16, stride=M), :] = current[c] * (factor[c] * keep)
            up = k + 1.0
            degree2 = 2.0 * (wave + up)
            coef = jnp.sqrt((degree2 * degree2 - 1.0) / (up * (2.0 * wave + up)))
            ratio = coef / last
            for c in range(2):
                following = (coef * cosines[c]) * current[c] - ratio * previous[c]
                previous[c] = current[c]
                current[c] = following
            last = coef
        for c in range(2):
            biggest = jnp.maximum(jnp.abs(current[c]), jnp.abs(previous[c]))
            shrink = 1.0 / biggest
            current[c] = current[c] * shrink
            previous[c] = previous[c] * shrink
            logs[c] = logs[c] + jnp.log(biggest)
        return tuple(current), tuple(previous), tuple(logs), last

    ones = jnp.ones((16, 128), F32)
    zeros = jnp.zeros((16, 128), F32)
    lax.fori_loop(0, M // 16, block, ((ones, ones), (zeros, zeros), (zeros, zeros), ones))

    old, new = iota((2 * COLS, 2 * COLS), 0), iota((2 * COLS, 2 * COLS), 1)
    perm = (reordered(old % COLS, new % COLS) & (old // COLS == new // COLS)).astype(BF16)

    def slot(j, _):
        for c in range(2):
            table_ref[j, :, c * 128 : (c + 1) * 128] = scratch[c, pl.ds(j * M, M), :].astype(BF16)
        keep, _ = keep_of(wave_smem[base + j])
        given = jnp.concatenate(
            [spectra_ref[j, pl.ds(parity, HK, stride=2), :] for parity in range(2)], axis=0
        )
        moved = dot(split(given), perm)
        high = moved[:, :COLS] * keep
        state_ref[j] = high + moved[:, COLS:] * keep
        legendre_rows(j, table_ref, high.astype(BF16), send_ref)
        return 0

    lax.fori_loop(0, SLOTS, slot, 0)


def update_kernel(last, wave_smem, table_ref, state_ref, rows_ref, mix_ref, speed_ref, *outs):
    base = lax.axis_index("space") * SLOTS
    speed = speed_ref[0:1, :]
    new, old = iota((2 * COLS, COLS), 0), iota((2 * COLS, COLS), 1)
    perm = reordered(old, new % COLS).astype(BF16)

    def slot(j, _):
        rows = jnp.concatenate(
            [
                jnp.concatenate([rows_ref[d, j] for d in range(SPACE // 2)], axis=0),
                jnp.concatenate([rows_ref[SPACE - 1 - d, j] for d in range(SPACE // 2)], axis=0),
            ],
            axis=1,
        )
        change = dot(table_ref[j], rows)
        north, south = change[:, :COLS], change[:, COLS:]
        change = jnp.concatenate([north[:HK] + south[:HK], north[HK:] - south[HK:]], axis=0)
        combined = state_ref[j] + change
        keep, degree = keep_of(wave_smem[base + j])
        stiffness = speed * (degree * (degree + 1)).astype(F32)
        damping = stiffness / (1.0 + stiffness)
        projected = dot(split(combined), mix_ref[0])
        projected = damping * (projected[:, :COLS] + projected[:, COLS:])
        returned = dot(split(projected), mix_ref[1])
        result = (combined - (returned[:, :COLS] + returned[:, COLS:])) * keep
        if last:
            result = dot(split(result), perm)
            for parity in range(2):
                outs[0][j, pl.ds(parity, HK, stride=2), :] = result[parity * HK : (parity + 1) * HK]
        else:
            outs[0][j] = result
            legendre_rows(j, table_ref, result.astype(BF16), outs[1])
        return 0

    lax.fori_loop(0, SLOTS, slot, 0)


def zonal_tables(wave_ref, synth_ref, analysis_ref):
    step = 2.0 * math.pi / NLON

    def angle_of(count):
        return (count - NLON * jnp.floor(count * (1.0 / NLON))) * step

    def rows(i, _):
        at = pl.ds(pl.multiple_of(i * 64, 64), 64)
        below = pl.ds(pl.multiple_of(M + i * 64, 64), 64)
        wave = wave_ref[at, :]
        x = iota((64, 128), 1).astype(F32)
        angle = angle_of(wave * x)
        turn = angle_of(wave * jnp.full((64, 128), 128.0, F32))
        cosine, sine = jnp.cos(angle), jnp.sin(angle)
        turn_cosine, turn_sine = jnp.cos(turn), jnp.sin(turn)
        factor = jnp.where(wave == 0.0, 1.0, 2.0)
        for c in range(CHUNKS):
            width = min(128, NLON - c * 128)
            lanes = slice(c * 128, c * 128 + width)
            synth_ref[at, lanes] = (factor * cosine)[:, :width].astype(BF16)
            synth_ref[below, lanes] = (-factor * sine)[:, :width].astype(BF16)
            analysis_ref[at, lanes] = (cosine * (1.0 / NLON))[:, :width].astype(BF16)
            analysis_ref[below, lanes] = (sine * (-1.0 / NLON))[:, :width].astype(BF16)
            cosine, sine = (
                cosine * turn_cosine - sine * turn_sine,
                sine * turn_cosine + cosine * turn_sine,
            )
        return 0

    lax.fori_loop(0, M // 64, rows, 0)


def grid_kernel(weight_smem, wave_ref, rows_ref, synth_ref, analysis_ref, traj_ref, out_ref, wide, narrow):
    g = pl.program_id(0)
    space = lax.axis_index("space")
    flip = space >= SPACE // 2
    first_weight = jnp.where(flip, SPACE - 1 - space, space) * LATS

    @pl.when(g == 0)
    def _():
        def widen(i, _):
            at = pl.ds(pl.multiple_of(i * 512, 512), 512)
            wide[at, :] = rows_ref[at, :].astype(F32)
            return 0

        lax.fori_loop(0, M * PAD // 512, widen, 0)

    wave = wave_ref[...]
    low = iota((M, COLS), 1) < ROWS
    values_in, slopes_in = [], []
    for pair in range(GROUP // 2):
        t = g * GROUP + 2 * pair
        one = wide[pl.ds(t, M, stride=PAD), :]
        two = wide[pl.ds(t + 1, M, stride=PAD), :]
        real = jnp.where(low, one, pltpu.roll(two, ROWS, 1))
        imag = jnp.where(low, pltpu.roll(one, ROWS, 1), two)
        values_in.append(jnp.concatenate([real, imag], axis=0).astype(BF16))
        slopes_in.append(jnp.concatenate([-wave * imag, wave * real], axis=0).astype(BF16))
    values = dot(jnp.concatenate(values_in, axis=1), synth_ref[...], ((0,), (0,)))
    slopes = dot(jnp.concatenate(slopes_in, axis=1), synth_ref[...], ((0,), (0,)))
    pieces = []
    for q in range(GROUP):
        i = jnp.minimum(g * GROUP + q, LATS - 1)
        t = jnp.where(flip, LATS - 1 - i, i)
        now = traj_ref[:, t].astype(F32)
        wind = jnp.concatenate([now[:, 0], now[:, 0]], axis=1)
        state = jnp.concatenate([now[:, 2], now[:, 1]], axis=1)
        v = values[q * ROWS : (q + 1) * ROWS].reshape(8, 8, NLON)
        s = slopes[q * ROWS : (q + 1) * ROWS].reshape(8, 8, NLON)
        forcing = (wind * s + state * v) * -weight_smem[first_weight + i]
        pieces.append(forcing.reshape(ROWS, NLON).astype(BF16))
    forcing = jnp.concatenate(pieces, axis=0)
    waves = dot(analysis_ref[...], forcing, ((1,), (1,)))
    for pair in range(GROUP // 2):
        t = g * GROUP + 2 * pair
        real = waves[0:M, pair * COLS : (pair + 1) * COLS]
        imag = waves[M : 2 * M, pair * COLS : (pair + 1) * COLS]
        narrow[pl.ds(t, M, stride=PAD), :] = jnp.where(low, real, pltpu.roll(imag, ROWS, 1))
        narrow[pl.ds(t + 1, M, stride=PAD), :] = jnp.where(low, pltpu.roll(real, ROWS, 1), imag)

    @pl.when(g == PAD // GROUP - 1)
    def _():
        def shrink(i, _):
            at = pl.ds(pl.multiple_of(i * 512, 512), 512)
            out_ref[at, :] = narrow[at, :].astype(BF16)
            return 0

        lax.fori_loop(0, M * PAD // 512, shrink, 0)


def remote(src, dst, send, recv, **to):
    return pltpu.make_async_remote_copy(
        src, dst, send, recv, device_id=to, device_id_type=MESH
    )


def exchange_kernel(step, tables, *refs):
    refs = list(refs)
    src = refs.pop(0)
    if step is not None:
        own_ref, part_ref = refs.pop(0), refs.pop(0)
    if tables:
        wave_ref = refs.pop(0)
    dst = refs.pop(0)
    if step is not None:
        full = refs.pop(0)
    if tables:
        synth_ref, analysis_ref = refs.pop(0), refs.pop(0)
    send_sem, recv_sem, ring_send, ring_recv, own_sem = refs

    me = lax.axis_index("space")
    pert = lax.axis_index("pert")
    half, y = pert // 4, lax.rem(pert, 4)
    after, before = half * 4 + lax.rem(y + 1, 4), half * 4 + lax.rem(y + 3, 4)
    barrier = pltpu.get_barrier_semaphore()

    def greet(i, _):
        pl.semaphore_signal(
            barrier, inc=1, device_id={"space": lax.rem(me + i, SPACE)}, device_id_type=MESH
        )
        return 0

    lax.fori_loop(1, SPACE, greet, 0)
    guests = SPACE - 1
    if step is not None:
        for neighbour in (after, before):
            pl.semaphore_signal(barrier, inc=1, device_id={"pert": neighbour}, device_id_type=MESH)
        guests += 2
    pl.semaphore_wait(barrier, guests)

    def copy(i):
        to = lax.rem(me + i, SPACE)
        return remote(src.at[to], dst.at[me], send_sem.at[i], recv_sem.at[i], space=to)

    def start(i, _):
        copy(i).start()
        return 0

    lax.fori_loop(1, SPACE, start, 0)
    local = [pltpu.make_async_copy(src.at[me], dst.at[me], own_sem.at[0])]
    ring = []
    if step is not None:
        blocks = ((own_ref.at[step], half * 4), (part_ref.at[step], (1 - half) * 4))
        for n, (block, group) in enumerate(blocks):
            here = full.at[group + y]
            local.append(pltpu.make_async_copy(block, here, own_sem.at[1 + n]))
            ring.append(remote(block, here, ring_send.at[2 * n], ring_recv.at[2 * n], pert=after))
            ring.append(remote(block, here, ring_send.at[2 * n + 1], ring_recv.at[2 * n + 1], pert=before))
        for c in ring:
            c.start()
    for c in local:
        c.start()
    if tables:
        zonal_tables(wave_ref, synth_ref, analysis_ref)
    passed = []
    if step is not None:
        cut = LATS // 2 + 1
        for n, (_, group) in enumerate(blocks):
            for way, (origin, rows, to) in enumerate((
                (group + lax.rem(y + 3, 4), pl.ds(0, cut), after),
                (group + lax.rem(y + 1, 4), pl.ds(cut, LATS - cut), before),
            )):
                ring[2 * n + way].wait_recv()
                piece = full.at[origin, rows]
                at = 4 + 2 * n + way
                passed.append(remote(piece, piece, ring_send.at[at], ring_recv.at[at], pert=to))
                passed[-1].start()

    def finish(i, _):
        origin = lax.rem(me - i + SPACE, SPACE)
        remote(
            src.at[origin], dst.at[origin], send_sem.at[i], recv_sem.at[i], space=origin
        ).wait_recv()
        copy(i).wait_send()
        return 0

    lax.fori_loop(1, SPACE, finish, 0)
    for c in ring:
        c.wait_send()
    for c in passed:
        c.wait()
    for c in local:
        c.wait()


VMEM = pl.BlockSpec(memory_space=pltpu.VMEM)
SMEM = pl.BlockSpec(memory_space=pltpu.SMEM)
ANY = pl.BlockSpec(memory_space=pl.ANY)
PARAMS = pltpu.CompilerParams(vmem_limit_bytes=56 * 2**20)


def exchange(number, x, step=None, own=None, part=None, wave_rows=None):
    given, in_specs = [x], [ANY]
    out_shape, out_specs = [jax.ShapeDtypeStruct(x.shape, x.dtype)], [ANY]
    if step is not None:
        given += [own, part]
        in_specs += [ANY, ANY]
        out_shape.append(jax.ShapeDtypeStruct((PERT,) + own.shape[1:], BF16))
        out_specs.append(ANY)
    if wave_rows is not None:
        given.append(wave_rows)
        in_specs.append(VMEM)
        out_shape += [jax.ShapeDtypeStruct((2 * M, NLON), BF16)] * 2
        out_specs += [VMEM] * 2
    tables = wave_rows is not None
    return pl.pallas_call(
        lambda *refs: exchange_kernel(step, tables, *refs),
        out_shape=out_shape,
        in_specs=in_specs,
        out_specs=out_specs,
        scratch_shapes=[
            pltpu.SemaphoreType.DMA((SPACE,)),
            pltpu.SemaphoreType.DMA((SPACE,)),
            pltpu.SemaphoreType.DMA((8,)),
            pltpu.SemaphoreType.DMA((8,)),
            pltpu.SemaphoreType.DMA((3,)),
        ],
        compiler_params=pltpu.CompilerParams(collective_id=number, has_side_effects=True),
        name="exchange",
    )(*given)


def grid_stage(weight, wave_rows, rows, synth, analysis, traj):
    whole = lambda shape: pl.BlockSpec(shape, lambda g: (0,) * len(shape), pipeline_mode=pl.Buffered(1))
    return pl.pallas_call(
        grid_kernel,
        grid=(PAD // GROUP,),
        out_shape=jax.ShapeDtypeStruct((M * PAD, COLS), BF16),
        in_specs=[
            SMEM,
            whole((M, 1)),
            whole((M * PAD, COLS)),
            whole((2 * M, NLON)),
            whole((2 * M, NLON)),
            whole((PERT, LATS, 3, 4, NLON)),
        ],
        out_specs=pl.BlockSpec((M * PAD, COLS), lambda g: (0, 0), pipeline_mode=pl.Buffered(1)),
        scratch_shapes=[pltpu.VMEM((M * PAD, COLS), F32), pltpu.VMEM((M * PAD, COLS), F32)],
        compiler_params=PARAMS,
        name="grid_stage",
    )(weight, wave_rows, rows, synth, analysis, traj)


def shards(spectra, wave_order, traj_wind, traj_state, vertical_modes, mode_speeds):
    lat_rows, weight = northern()
    fields = jnp.concatenate([traj_wind[:, None], traj_state], axis=1)
    fields = jnp.transpose(fields, (0, 3, 1, 2, 4))
    partner = lax.ppermute(fields, "pert", [(p, (p + 4) % PERT) for p in range(PERT)])
    wave_rows = wave_order.astype(F32)[:, None]

    send_shape = jax.ShapeDtypeStruct((SPACE, SLOTS, PAD, COLS), BF16)
    state_shape = jax.ShapeDtypeStruct((SLOTS, M, COLS), F32)
    table, state, send, mix, speed = pl.pallas_call(
        table_kernel,
        out_shape=(
            jax.ShapeDtypeStruct((SLOTS, M, HALF), BF16),
            state_shape,
            send_shape,
            jax.ShapeDtypeStruct((2, 2 * COLS, 2 * COLS), BF16),
            jax.ShapeDtypeStruct((8, COLS), F32),
        ),
        in_specs=[SMEM] + [VMEM] * 4,
        out_specs=(VMEM,) * 5,
        scratch_shapes=[pltpu.VMEM((2, 16 * M, 128), F32)],
        compiler_params=PARAMS,
        cost_estimate=pl.CostEstimate(flops=10**10, bytes_accessed=3 * 10**7, transcendentals=10**6),
        name="table_stage",
    )(wave_order, jnp.asarray(lat_rows), spectra, vertical_modes, mode_speeds[None])

    for step in range(STEPS):
        if step == 0:
            rows, traj, synth, analysis = exchange(1, send, 0, fields, partner, wave_rows)
        else:
            rows = exchange(3, send)[0]
        waves = grid_stage(jnp.asarray(weight), wave_rows, rows.reshape(M * PAD, COLS), synth, analysis, traj)
        waves = waves.reshape(SPACE, SLOTS, PAD, COLS)
        if step == 0:
            back, traj = exchange(2, waves, 1, fields, partner)
        else:
            back = exchange(3, waves)[0]
        last = step == STEPS - 1
        result = pl.pallas_call(
            lambda *refs, last=last: update_kernel(last, *refs),
            out_shape=state_shape if last else (state_shape, send_shape),
            in_specs=[SMEM] + [VMEM] * 5,
            out_specs=VMEM if last else (VMEM, VMEM),
            compiler_params=PARAMS,
            name="last_update" if last else "update",
        )(wave_order, table, state, back, mix, speed)
        if last:
            return result
        state, send = result


def solution(mesh):
    placed = (
        P("space", None, "pert"),
        P(),
        P(None, "pert", "space", None),
        P(None, None, "pert", "space", None),
        P(),
        P(),
    )
    return jax.shard_map(
        shards, mesh=mesh, in_specs=placed, out_specs=P("space", None, "pert"), check_vma=False
    )
```

```python
import math

import jax
import jax.numpy as jnp
import numpy as np
from jax import lax
from jax.experimental import pallas as pl
from jax.experimental.pallas import tpu as pltpu
from jax.sharding import PartitionSpec as P

NLAT = 480
NLON = 960
M = 320
VARS = 2
LEV = 32
STEPS = 2
PERT = 8
SPACE = 32
SLOTS = M // SPACE
LATS = NLAT // SPACE
PAD = 16
HALF = (SPACE // 2) * PAD
COLS = 128
ROWS = COLS // 2
HK = M // 2
PART = PAD // 2
CHUNKS = 8
GROUP = 4
F32 = jnp.float32
BF16 = jnp.bfloat16
MESH = pl.DeviceIdType.MESH
HIGHEST = lax.Precision.HIGHEST


def dot(a, b, dims=((1,), (0,)), precision=None):
    return lax.dot_general(
        a, b, (dims, ((), ())), preferred_element_type=F32, precision=precision
    )


def iota(shape, axis):
    return lax.broadcasted_iota(jnp.int32, shape, axis)


def level_of(new):
    return new % ROWS // 8 * 4 + new % 4


def group_of(new):
    return new // ROWS * 2 + new % 8 // 4


def reordered(old, new):
    return old == new % 8 // 4 * 64 + level_of(new) * 2 + new // ROWS


def split(x):
    high = x.astype(BF16)
    return jnp.concatenate([high, (x - high.astype(F32)).astype(BF16)], axis=1)


def northern():
    place = np.arange(HALF)
    row = place // COLS * PART + place % PART
    inside = row < LATS
    lat = np.minimum(place % COLS // PART * LATS + row, NLAT // 2 - 1)
    angle = (lat + 0.5) * (math.pi / NLAT)
    rows = np.stack([np.cos(angle), np.log(np.sin(angle)), inside.astype(np.float64)])
    weight = np.sin((np.arange(NLAT // 2) + 0.5) * (math.pi / NLAT)) * (math.pi / NLAT)
    return rows.astype(np.float32), weight.astype(np.float32)


def keep_of(w):
    row = iota((M, COLS), 0)
    degree = jnp.where(row < HK, 2 * row, 2 * row - (M - 1)) + w
    keep = (degree <= M - 1) & jnp.logical_not((iota((M, COLS), 1) >= ROWS) & (w == 0))
    return keep.astype(F32), degree


def legendre_rows(j, table_ref, state, send_ref):
    even, odd = state[:HK], state[HK:]
    both = jnp.concatenate(
        [jnp.concatenate([even, even], axis=1), jnp.concatenate([odd, -odd], axis=1)], axis=0
    )
    rows = dot(table_ref[j], both, ((0,), (0,)))
    for half in range(2):
        for d in range(SPACE // 2):
            at = half * COLS + d * PART
            send_ref[half, d, j] = rows[at : at + PART, :COLS].astype(BF16)
            send_ref[half, SPACE - 1 - d, j] = rows[at : at + PART, COLS:].astype(BF16)


def table_kernel(
    wave_smem, lat_ref, spectra_ref, modes_ref, speeds_ref,
    table_ref, state_ref, send_ref, mix_ref, speed_ref, scratch,
):
    lev = iota((LEV, COLS), 0)
    onehot = (level_of(iota((LEV, COLS), 1)) == lev).astype(F32)
    same = (group_of(iota((COLS, COLS), 0)) == group_of(iota((COLS, COLS), 1))).astype(F32)
    for way in range(2):
        spread = dot(onehot, modes_ref[...], ((0,), (1 - way,)), HIGHEST)
        mix = dot(spread, onehot, precision=HIGHEST) * same
        high = mix.astype(BF16)
        low = (mix - high.astype(F32)).astype(BF16)
        mix_ref[way, :COLS, :COLS] = high
        mix_ref[way, :COLS, COLS:] = low
        mix_ref[way, COLS:, :COLS] = high
        mix_ref[way, COLS:, COLS:] = jnp.zeros_like(low)
    speed_ref[...] = dot(jnp.broadcast_to(speeds_ref[...], (8, LEV)), onehot, precision=HIGHEST)

    base = lax.axis_index("space") * SLOTS
    row16 = iota((16, 128), 0)
    wave = jnp.zeros((16, 128), jnp.int32)
    for j in range(SLOTS):
        wave = jnp.where(row16 == j, wave_smem[base + j], wave)
    wave = wave.astype(F32)
    cosines = [lat_ref[0:1, c * 128 : (c + 1) * 128] for c in range(2)]
    number = (iota((16, 384), 1) + 1).astype(F32)
    terms = jnp.where(number <= wave[:, 0:1], jnp.log((2.0 * number + 1.0) / (2.0 * number)), 0.0)
    start = 0.5 * jnp.sum(terms, axis=1, keepdims=True) - 0.5 * math.log(2.0)
    starts = [start + wave * lat_ref[1:2, c * 128 : (c + 1) * 128] for c in range(2)]
    inside = [lat_ref[2:3, c * 128 : (c + 1) * 128] for c in range(2)]

    def block(b, carry):
        current, previous, logs, last = carry
        current, previous, logs = list(current), list(previous), list(logs)
        factor = [jnp.exp(starts[c] + logs[c]) * inside[c] for c in range(2)]
        first = b * 16
        for i in range(16):
            k = (first + i).astype(F32)
            keep = (wave + k <= M - 1.0).astype(F32)
            row = (i % 2) * HK + b * 8 + i // 2
            for c in range(2):
                scratch[c, pl.ds(row, 16, stride=M), :] = current[c] * (factor[c] * keep)
            up = k + 1.0
            degree2 = 2.0 * (wave + up)
            coef = jnp.sqrt((degree2 * degree2 - 1.0) / (up * (2.0 * wave + up)))
            ratio = coef / last
            for c in range(2):
                following = (coef * cosines[c]) * current[c] - ratio * previous[c]
                previous[c] = current[c]
                current[c] = following
            last = coef
        for c in range(2):
            biggest = jnp.maximum(jnp.abs(current[c]), jnp.abs(previous[c]))
            shrink = 1.0 / biggest
            current[c] = current[c] * shrink
            previous[c] = previous[c] * shrink
            logs[c] = logs[c] + jnp.log(biggest)
        return tuple(current), tuple(previous), tuple(logs), last

    ones = jnp.ones((16, 128), F32)
    zeros = jnp.zeros((16, 128), F32)
    lax.fori_loop(0, M // 16, block, ((ones, ones), (zeros, zeros), (zeros, zeros), ones))

    old, new = iota((2 * COLS, 2 * COLS), 0), iota((2 * COLS, 2 * COLS), 1)
    perm = (reordered(old % COLS, new % COLS) & (old // COLS == new // COLS)).astype(BF16)

    def slot(j, _):
        for c in range(2):
            table_ref[j, :, c * 128 : (c + 1) * 128] = scratch[c, pl.ds(j * M, M), :].astype(BF16)
        keep, _ = keep_of(wave_smem[base + j])
        given = jnp.concatenate(
            [spectra_ref[j, pl.ds(parity, HK, stride=2), :] for parity in range(2)], axis=0
        )
        moved = dot(split(given), perm)
        high = moved[:, :COLS] * keep
        state_ref[j] = high + moved[:, COLS:] * keep
        legendre_rows(j, table_ref, high.astype(BF16), send_ref)
        return 0

    lax.fori_loop(0, SLOTS, slot, 0)


def updated(j, w, table_ref, state_ref, rows_ref, mix_ref, speed):
    sides = []
    for order in (lambda d: d, lambda d: SPACE - 1 - d):
        pieces = [
            rows_ref[half, order(d), j].astype(F32) for half in range(2) for d in range(SPACE // 2)
        ]
        sides.append(jnp.concatenate(pieces, axis=0).astype(BF16))
    change = dot(table_ref[j], jnp.concatenate(sides, axis=1))
    north, south = change[:, :COLS], change[:, COLS:]
    change = jnp.concatenate([north[:HK] + south[:HK], north[HK:] - south[HK:]], axis=0)
    combined = state_ref[j] + change
    keep, degree = keep_of(w)
    stiffness = speed * (degree * (degree + 1)).astype(F32)
    damping = stiffness / (1.0 + stiffness)
    projected = dot(split(combined), mix_ref[0])
    projected = damping * (projected[:, :COLS] + projected[:, COLS:])
    returned = dot(split(projected), mix_ref[1])
    return (combined - (returned[:, :COLS] + returned[:, COLS:])) * keep


def update_kernel(wave_smem, table_ref, state_ref, rows_ref, mix_ref, speed_ref, out_ref):
    base = lax.axis_index("space") * SLOTS
    speed = speed_ref[0:1, :]
    new, old = iota((2 * COLS, COLS), 0), iota((2 * COLS, COLS), 1)
    perm = reordered(old, new % COLS).astype(BF16)

    def slot(j, _):
        result = updated(j, wave_smem[base + j], table_ref, state_ref, rows_ref, mix_ref, speed)
        result = dot(split(result), perm)
        for parity in range(2):
            out_ref[j, pl.ds(parity, HK, stride=2), :] = result[parity * HK : (parity + 1) * HK]
        return 0

    lax.fori_loop(0, SLOTS, slot, 0)


def zonal_tables(wave_ref, synth_ref, analysis_ref):
    step = 2.0 * math.pi / NLON

    def angle_of(count):
        return (count - NLON * jnp.floor(count * (1.0 / NLON))) * step

    def rows(i, _):
        at = pl.ds(pl.multiple_of(i * 64, 64), 64)
        below = pl.ds(pl.multiple_of(M + i * 64, 64), 64)
        wave = wave_ref[at, :]
        x = iota((64, 128), 1).astype(F32)
        angle = angle_of(wave * x)
        turn = angle_of(wave * jnp.full((64, 128), 128.0, F32))
        cosine, sine = jnp.cos(angle), jnp.sin(angle)
        turn_cosine, turn_sine = jnp.cos(turn), jnp.sin(turn)
        factor = jnp.where(wave == 0.0, 1.0, 2.0)
        for c in range(CHUNKS):
            width = min(128, NLON - c * 128)
            lanes = slice(c * 128, c * 128 + width)
            synth_ref[at, lanes] = (factor * cosine)[:, :width].astype(BF16)
            synth_ref[below, lanes] = (-factor * sine)[:, :width].astype(BF16)
            analysis_ref[at, lanes] = (cosine * (1.0 / NLON))[:, :width].astype(BF16)
            analysis_ref[below, lanes] = (sine * (-1.0 / NLON))[:, :width].astype(BF16)
            cosine, sine = (
                cosine * turn_cosine - sine * turn_sine,
                sine * turn_cosine + cosine * turn_sine,
            )
        return 0

    lax.fori_loop(0, M // 64, rows, 0)


def grid_half(half, weight_smem, wave_ref, rows_ref, synth_ref, analysis_ref, traj_ref, out_ref, wide, narrow):
    space = lax.axis_index("space")
    flip = space >= SPACE // 2
    first_weight = jnp.where(flip, SPACE - 1 - space, space) * LATS

    def widen(n, _):
        at = pl.ds(pl.multiple_of(n * (SLOTS * PART), SLOTS * PART), SLOTS * PART)
        wide[at, :] = rows_ref[n].astype(F32).reshape(SLOTS * PART, COLS)
        return 0

    lax.fori_loop(0, SPACE, widen, 0)
    wave = wave_ref[...]
    low = iota((M, COLS), 1) < ROWS

    def group(g, _):
        values_in, slopes_in = [], []
        for pair in range(GROUP // 2):
            t = g * GROUP + 2 * pair
            one = wide[pl.ds(t, M, stride=PART), :]
            two = wide[pl.ds(t + 1, M, stride=PART), :]
            real = jnp.where(low, one, pltpu.roll(two, ROWS, 1))
            imag = jnp.where(low, pltpu.roll(one, ROWS, 1), two)
            values_in.append(jnp.concatenate([real, imag], axis=0).astype(BF16))
            slopes_in.append(jnp.concatenate([-wave * imag, wave * real], axis=0).astype(BF16))
        values = dot(jnp.concatenate(values_in, axis=1), synth_ref[...], ((0,), (0,)))
        slopes = dot(jnp.concatenate(slopes_in, axis=1), synth_ref[...], ((0,), (0,)))
        pieces = []
        for q in range(GROUP):
            i = jnp.minimum(half * PART + g * GROUP + q, LATS - 1)
            t = jnp.where(flip, LATS - 1 - i, i)
            now = traj_ref[:, t].astype(F32)
            wind = jnp.concatenate([now[:, 0], now[:, 0]], axis=1)
            state = jnp.concatenate([now[:, 2], now[:, 1]], axis=1)
            v = values[q * ROWS : (q + 1) * ROWS].reshape(8, 8, NLON)
            s = slopes[q * ROWS : (q + 1) * ROWS].reshape(8, 8, NLON)
            forcing = (wind * s + state * v) * -weight_smem[first_weight + i]
            pieces.append(forcing.reshape(ROWS, NLON).astype(BF16))
        forcing = jnp.concatenate(pieces, axis=0)
        waves = dot(analysis_ref[...], forcing, ((1,), (1,)))
        for pair in range(GROUP // 2):
            t = g * GROUP + 2 * pair
            real = waves[0:M, pair * COLS : (pair + 1) * COLS]
            imag = waves[M : 2 * M, pair * COLS : (pair + 1) * COLS]
            narrow[pl.ds(t, M, stride=PART), :] = jnp.where(low, real, pltpu.roll(imag, ROWS, 1))
            narrow[pl.ds(t + 1, M, stride=PART), :] = jnp.where(low, pltpu.roll(real, ROWS, 1), imag)
        return 0

    lax.fori_loop(0, PART // GROUP, group, 0)

    def shrink(n, _):
        at = pl.ds(pl.multiple_of(n * (SLOTS * PART), SLOTS * PART), SLOTS * PART)
        out_ref[n] = narrow[at, :].reshape(SLOTS, PART, COLS).astype(BF16)
        return 0

    lax.fori_loop(0, SPACE, shrink, 0)


def remote(src, dst, send, recv, **to):
    return pltpu.make_async_remote_copy(
        src, dst, send, recv, device_id=to, device_id_type=MESH
    )


def steps_kernel(
    wave_smem, weight_smem, wave_ref, table_ref, state_ref, mix_ref, speed_ref, first_ref, own_ref, part_ref,
    back_ref, result_ref,
    traj, synth, analysis, there_0, there_1, grid_0, grid_1, back_0, second, wide, narrow,
    send_sem, recv_sem, own_sem, ring_send, ring_recv, ring_own,
):
    me = lax.axis_index("space")
    pert = lax.axis_index("pert")
    side, y = pert // 4, lax.rem(pert, 4)
    after, before = side * 4 + lax.rem(y + 1, 4), side * 4 + lax.rem(y + 3, 4)
    barrier = pltpu.get_barrier_semaphore()

    def greet(i, _):
        pl.semaphore_signal(
            barrier, inc=1, device_id={"space": lax.rem(me + i, SPACE)}, device_id_type=MESH
        )
        return 0

    lax.fori_loop(1, SPACE, greet, 0)
    for neighbour in (after, before):
        pl.semaphore_signal(barrier, inc=1, device_id={"pert": neighbour}, device_id_type=MESH)
    pl.semaphore_wait(barrier, SPACE + 1)

    exchanges = ((first_ref, there_0), (grid_0, back_0), (second, there_1), (grid_1, back_ref))

    def own_copy(e, chunk, half, slots):
        src, dst = exchanges[e]
        return pltpu.make_async_copy(
            src.at[half, me, slots], dst.at[half, me, slots], own_sem.at[e, chunk]
        )

    def push(e, chunk, half, slots=pl.ds(0, SLOTS)):
        src, dst = exchanges[e]

        def start(i, _):
            to = lax.rem(me + i, SPACE)
            remote(
                src.at[half, to, slots], dst.at[half, me, slots],
                send_sem.at[e, chunk], recv_sem.at[e, chunk], space=to,
            ).start()
            return 0

        lax.fori_loop(1, SPACE, start, 0)
        own_copy(e, chunk, half, slots).start()

    def everyone(e, chunk, half, slots):
        src, dst = exchanges[e]
        others = pl.ds(0, SPACE - 1)
        return remote(
            src.at[half, others, slots], dst.at[half, others, slots],
            send_sem.at[e, chunk], recv_sem.at[e, chunk], space=lax.rem(me + 1, SPACE),
        )

    def arrive(e, chunk, half, slots=pl.ds(0, SLOTS)):
        everyone(e, chunk, half, slots).wait_recv()
        own_copy(e, chunk, half, slots).wait()

    def drain(e, chunk, half, slots=pl.ds(0, SLOTS)):
        everyone(e, chunk, half, slots).wait_send()

    for half in range(2):
        push(0, half, half)
    rings, locals_ = [], []
    for step in range(STEPS):
        for n, (block, group) in enumerate(
            ((own_ref.at[step], side * 4), (part_ref.at[step], (1 - side) * 4))
        ):
            here = traj.at[step, group + y]
            locals_.append(pltpu.make_async_copy(block, here, ring_own.at[step, n]))
            for way, to in enumerate((after, before)):
                at = 2 * n + way
                rings.append(remote(block, here, ring_send.at[step, at], ring_recv.at[step, at], pert=to))
    for c in rings + locals_:
        c.start()
    passed = []

    def pass_on(step):
        cut = LATS // 2 + 1
        for n, group in enumerate((side * 4, (1 - side) * 4)):
            for way, (origin, rows, to) in enumerate((
                (group + lax.rem(y + 3, 4), pl.ds(0, cut), after),
                (group + lax.rem(y + 1, 4), pl.ds(cut, LATS - cut), before),
            )):
                rings[4 * step + 2 * n + way].wait_recv()
                piece = traj.at[step, origin, rows]
                at = 4 + 2 * n + way
                passed.append(
                    remote(piece, piece, ring_send.at[step, at], ring_recv.at[step, at], pert=to)
                )
                passed[-1].start()

    zonal_tables(wave_ref, synth, analysis)
    pass_on(0)
    speed = speed_ref[0:1, :]
    base = me * SLOTS

    def slot(j, _):
        result = updated(j, wave_smem[base + j], table_ref, state_ref, back_0, mix_ref, speed)
        result_ref[j] = result
        legendre_rows(j, table_ref, result.astype(BF16), second)
        return 0

    few = SLOTS // 2
    early, late = pl.ds(0, few), pl.ds(few, few)
    for step in range(STEPS):
        rows, out = (there_0, grid_0) if step == 0 else (there_1, grid_1)
        for half in range(2):
            if step == 0:
                arrive(0, half, half)
            else:
                arrive(2, half, half, early)
                arrive(2, 2 + half, half, late)
            if half == 0:
                for c in passed[4 * step :]:
                    c.wait_recv()
                for c in locals_[2 * step : 2 * step + 2]:
                    c.wait()
            grid_half(
                half, weight_smem, wave_ref, rows.at[half], synth, analysis, traj.at[step], out.at[half], wide, narrow
            )
            push(2 * step + 1, half, half)
        if step == 0:
            pass_on(1)
            for half in range(2):
                arrive(1, half, half)
            lax.fori_loop(0, few, slot, 0)
            push(2, 0, 0, early)
            lax.fori_loop(few, SLOTS, slot, 0)
            push(2, 2, 0, late)
            push(2, 1, 1, early)
            push(2, 3, 1, late)
    for half in range(2):
        arrive(3, half, half)
    for e in (0, 1, 3):
        for half in range(2):
            drain(e, half, half)
    for half in range(2):
        drain(2, half, half, early)
        drain(2, 2 + half, half, late)
    for c in rings + passed:
        c.wait_send()


VMEM = pl.BlockSpec(memory_space=pltpu.VMEM)
SMEM = pl.BlockSpec(memory_space=pltpu.SMEM)
ANY = pl.BlockSpec(memory_space=pl.ANY)
PARAMS = pltpu.CompilerParams(vmem_limit_bytes=60 * 2**20)


def shards(spectra, wave_order, traj_wind, traj_state, vertical_modes, mode_speeds):
    lat_rows, weight = northern()
    fields = jnp.concatenate([traj_wind[:, None], traj_state], axis=1)
    fields = jnp.transpose(fields, (0, 3, 1, 2, 4))
    partner = lax.ppermute(fields, "pert", [(p, (p + 4) % PERT) for p in range(PERT)])
    wave_rows = wave_order.astype(F32)[:, None]

    rows_shape = (2, SPACE, SLOTS, PART, COLS)
    send_shape = jax.ShapeDtypeStruct(rows_shape, BF16)
    state_shape = jax.ShapeDtypeStruct((SLOTS, M, COLS), F32)
    table, state, send, mix, speed = pl.pallas_call(
        table_kernel,
        out_shape=(
            jax.ShapeDtypeStruct((SLOTS, M, HALF), BF16),
            state_shape,
            send_shape,
            jax.ShapeDtypeStruct((2, 2 * COLS, 2 * COLS), BF16),
            jax.ShapeDtypeStruct((8, COLS), F32),
        ),
        in_specs=[SMEM] + [VMEM] * 4,
        out_specs=(VMEM,) * 5,
        scratch_shapes=[pltpu.VMEM((2, 16 * M, 128), F32)],
        compiler_params=PARAMS,
        cost_estimate=pl.CostEstimate(flops=10**10, bytes_accessed=3 * 10**7, transcendentals=10**6),
        name="table_stage",
    )(wave_order, jnp.asarray(lat_rows), spectra, vertical_modes, mode_speeds[None])
    back, state = pl.pallas_call(
        steps_kernel,
        out_shape=(send_shape, state_shape),
        in_specs=[SMEM] * 2 + [VMEM] * 5 + [ANY] * 3,
        out_specs=(ANY, VMEM),
        scratch_shapes=[
            pltpu.VMEM((STEPS, PERT, LATS, 3, 4, NLON), BF16),
            pltpu.VMEM((2 * M, NLON), BF16),
            pltpu.VMEM((2 * M, NLON), BF16),
        ]
        + [pltpu.VMEM(rows_shape, BF16)] * 6
        + [pltpu.VMEM((M * PART, COLS), F32)] * 2
        + [pltpu.SemaphoreType.DMA((4, 4))] * 3
        + [pltpu.SemaphoreType.DMA((STEPS, 8))] * 2
        + [pltpu.SemaphoreType.DMA((STEPS, 2))],
        compiler_params=pltpu.CompilerParams(
            collective_id=1, has_side_effects=True, vmem_limit_bytes=60 * 2**20
        ),
        name="steps",
    )(wave_order, jnp.asarray(weight), wave_rows, table, state, mix, speed, send, fields, partner)
    return pl.pallas_call(
        update_kernel,
        out_shape=state_shape,
        in_specs=[SMEM] + [VMEM] * 5,
        out_specs=VMEM,
        compiler_params=PARAMS,
        name="last_update",
    )(wave_order, table, state, back, mix, speed)


def solution(mesh):
    placed = (
        P("space", None, "pert"),
        P(),
        P(None, "pert", "space", None),
        P(None, None, "pert", "space", None),
        P(),
        P(),
    )
    return jax.shard_map(
        shards, mesh=mesh, in_specs=placed, out_specs=P("space", None, "pert"), check_vma=False
    )
```

```python
import math

import jax
import jax.numpy as jnp
import numpy as np
from jax import lax
from jax.experimental import pallas as pl
from jax.experimental.pallas import tpu as pltpu
from jax.sharding import PartitionSpec as P

NLAT = 480
NLON = 960
M = 320
VARS = 2
LEV = 32
STEPS = 2
PERT = 8
SPACE = 32
SLOTS = M // SPACE
LATS = NLAT // SPACE
PAD = 16
HALF = (SPACE // 2) * PAD
COLS = 128
ROWS = COLS // 2
HK = M // 2
PART = PAD // 2
CHUNKS = 8
GROUP = 4
F32 = jnp.float32
BF16 = jnp.bfloat16
MESH = pl.DeviceIdType.MESH
HIGHEST = lax.Precision.HIGHEST


def dot(a, b, dims=((1,), (0,)), precision=None):
    return lax.dot_general(
        a, b, (dims, ((), ())), preferred_element_type=F32, precision=precision
    )


def iota(shape, axis):
    return lax.broadcasted_iota(jnp.int32, shape, axis)


def level_of(new):
    return new % ROWS // 8 * 4 + new % 4


def group_of(new):
    return new // ROWS * 2 + new % 8 // 4


def reordered(old, new):
    return old == new % 8 // 4 * 64 + level_of(new) * 2 + new // ROWS


def split(x):
    high = x.astype(BF16)
    return jnp.concatenate([high, (x - high.astype(F32)).astype(BF16)], axis=1)


def northern():
    place = np.arange(HALF)
    row = place // COLS * PART + place % PART
    inside = row < LATS
    lat = np.minimum(place % COLS // PART * LATS + row, NLAT // 2 - 1)
    angle = (lat + 0.5) * (math.pi / NLAT)
    rows = np.stack([np.cos(angle), np.log(np.sin(angle)), inside.astype(np.float64)])
    weight = np.sin((np.arange(NLAT // 2) + 0.5) * (math.pi / NLAT)) * (math.pi / NLAT)
    return rows.astype(np.float32), weight.astype(np.float32)


def keep_of(w):
    row = iota((M, COLS), 0)
    degree = jnp.where(row < HK, 2 * row, 2 * row - (M - 1)) + w
    keep = (degree <= M - 1) & jnp.logical_not((iota((M, COLS), 1) >= ROWS) & (w == 0))
    return keep.astype(F32), degree


def legendre_rows(j, table_ref, state, send_ref):
    even, odd = state[:HK], state[HK:]
    both = jnp.concatenate(
        [jnp.concatenate([even, even], axis=1), jnp.concatenate([odd, -odd], axis=1)], axis=0
    )
    rows = dot(table_ref[j], both, ((0,), (0,)))
    for half in range(2):
        for d in range(SPACE // 2):
            at = half * COLS + d * PART
            send_ref[half, d, j] = rows[at : at + PART, :COLS].astype(BF16)
            send_ref[half, SPACE - 1 - d, j] = rows[at : at + PART, COLS:].astype(BF16)


def table_kernel(
    wave_smem, lat_ref, spectra_ref, modes_ref, speeds_ref,
    table_ref, state_ref, send_ref, mix_ref, speed_ref, scratch, coefs,
):
    lev = iota((LEV, COLS), 0)
    onehot = (level_of(iota((LEV, COLS), 1)) == lev).astype(F32)
    same = (group_of(iota((COLS, COLS), 0)) == group_of(iota((COLS, COLS), 1))).astype(F32)
    for way in range(2):
        spread = dot(onehot, modes_ref[...], ((0,), (1 - way,)), HIGHEST)
        mix = dot(spread, onehot, precision=HIGHEST) * same
        high = mix.astype(BF16)
        low = (mix - high.astype(F32)).astype(BF16)
        mix_ref[way, :COLS, :COLS] = high
        mix_ref[way, :COLS, COLS:] = low
        mix_ref[way, COLS:, :COLS] = high
        mix_ref[way, COLS:, COLS:] = jnp.zeros_like(low)
    speed_ref[...] = dot(jnp.broadcast_to(speeds_ref[...], (8, LEV)), onehot, precision=HIGHEST)

    base = lax.axis_index("space") * SLOTS
    row16 = iota((16, 128), 0)
    wave = jnp.zeros((16, 128), jnp.int32)
    for j in range(SLOTS):
        wave = jnp.where(row16 == j, wave_smem[base + j], wave)
    wave = wave.astype(F32)
    cosines = [lat_ref[0:1, c * 128 : (c + 1) * 128] for c in range(2)]
    number = (iota((16, 384), 1) + 1).astype(F32)
    terms = jnp.where(number <= wave[:, 0:1], jnp.log((2.0 * number + 1.0) / (2.0 * number)), 0.0)
    start = 0.5 * jnp.sum(terms, axis=1, keepdims=True) - 0.5 * math.log(2.0)
    starts = [start + wave * lat_ref[1:2, c * 128 : (c + 1) * 128] for c in range(2)]
    inside = [lat_ref[2:3, c * 128 : (c + 1) * 128] for c in range(2)]

    def coefficient(up, w):
        return jnp.sqrt((4.0 * (w + up) * (w + up) - 1.0) / (up * (2.0 * w + up)))

    for c in range(3):
        up = (iota((16, 128), 1) + (c * 128 + 1)).astype(F32)
        coefs[0, c] = coefficient(up, wave)
        coefs[1, c] = coefs[0, c] / coefficient(jnp.maximum(up - 1.0, 1.0), wave)

    def block(b, carry):
        current, previous, logs = (list(x) for x in carry)
        factor = [jnp.exp(starts[c] + logs[c]) * inside[c] for c in range(2)]
        shift = lax.rem(128 - 16 * lax.rem(b, 8), 128)
        coef, ratio = (pltpu.roll(coefs[n, b // 8], shift, 1) for n in range(2))
        for i in range(16):
            row = (i % 2) * HK + b * 8 + i // 2
            up, down = (jnp.broadcast_to(x[:, i : i + 1], (16, 128)) for x in (coef, ratio))
            for c in range(2):
                scratch[c, pl.ds(row, 16, stride=M), :] = current[c] * factor[c]
                following = (up * cosines[c]) * current[c] - down * previous[c]
                previous[c] = current[c]
                current[c] = following
        for c in range(2):
            biggest = jnp.maximum(jnp.abs(current[c]), jnp.abs(previous[c]))
            shrink = 1.0 / biggest
            current[c] = current[c] * shrink
            previous[c] = previous[c] * shrink
            logs[c] = logs[c] + jnp.log(biggest)
        return tuple(current), tuple(previous), tuple(logs)

    ones = jnp.ones((16, 128), F32)
    zeros = jnp.zeros((16, 128), F32)
    lax.fori_loop(0, M // 16, block, ((ones, ones), (zeros, zeros), (zeros, zeros)))

    old, new = iota((2 * COLS, 2 * COLS), 0), iota((2 * COLS, 2 * COLS), 1)
    perm = (reordered(old % COLS, new % COLS) & (old // COLS == new // COLS)).astype(BF16)

    def slot(j):
        for c in range(2):
            table_ref[j, :, c * 128 : (c + 1) * 128] = scratch[c, pl.ds(j * M, M), :].astype(BF16)
        keep, _ = keep_of(wave_smem[base + j])
        given = jnp.concatenate(
            [spectra_ref[j, pl.ds(parity, HK, stride=2), :] for parity in range(2)], axis=0
        )
        moved = dot(split(given), perm)
        high = moved[:, :COLS] * keep
        state_ref[j] = high + moved[:, COLS:] * keep
        legendre_rows(j, table_ref, high.astype(BF16), send_ref)

    def pair(n, _):
        slot(2 * n)
        slot(2 * n + 1)
        return 0

    lax.fori_loop(0, SLOTS // 2, pair, 0)


def updated(j, w, table_ref, state_ref, rows_ref, mix_ref, speed):
    sides = []
    for order in (lambda d: d, lambda d: SPACE - 1 - d):
        pieces = [
            rows_ref[half, order(d), j].astype(F32) for half in range(2) for d in range(SPACE // 2)
        ]
        sides.append(jnp.concatenate(pieces, axis=0).astype(BF16))
    change = dot(table_ref[j], jnp.concatenate(sides, axis=1))
    north, south = change[:, :COLS], change[:, COLS:]
    change = jnp.concatenate([north[:HK] + south[:HK], north[HK:] - south[HK:]], axis=0)
    combined = state_ref[j] + change
    keep, degree = keep_of(w)
    stiffness = speed * (degree * (degree + 1)).astype(F32)
    damping = stiffness / (1.0 + stiffness)
    projected = dot(split(combined), mix_ref[0])
    projected = damping * (projected[:, :COLS] + projected[:, COLS:])
    returned = dot(split(projected), mix_ref[1])
    return (combined - (returned[:, :COLS] + returned[:, COLS:])) * keep


def zonal_tables(wave_ref, synth_ref, analysis_ref):
    step = 2.0 * math.pi / NLON

    def angle_of(count):
        return (count - NLON * jnp.floor(count * (1.0 / NLON))) * step

    def rows(i, _):
        at = pl.ds(pl.multiple_of(i * 64, 64), 64)
        below = pl.ds(pl.multiple_of(M + i * 64, 64), 64)
        wave = wave_ref[at, :]
        x = iota((64, 128), 1).astype(F32)
        angle = angle_of(wave * x)
        turn = angle_of(wave * jnp.full((64, 128), 128.0, F32))
        cosine, sine = jnp.cos(angle), jnp.sin(angle)
        turn_cosine, turn_sine = jnp.cos(turn), jnp.sin(turn)
        factor = jnp.where(wave == 0.0, 1.0, 2.0)
        for c in range(CHUNKS):
            width = min(128, NLON - c * 128)
            lanes = slice(c * 128, c * 128 + width)
            synth_ref[at, lanes] = (factor * cosine)[:, :width].astype(BF16)
            synth_ref[below, lanes] = (-factor * sine)[:, :width].astype(BF16)
            analysis_ref[at, lanes] = (cosine * (1.0 / NLON))[:, :width].astype(BF16)
            analysis_ref[below, lanes] = (sine * (-1.0 / NLON))[:, :width].astype(BF16)
            cosine, sine = (
                cosine * turn_cosine - sine * turn_sine,
                sine * turn_cosine + cosine * turn_sine,
            )
        return 0

    lax.fori_loop(0, M // 64, rows, 0)


def grid_half(half, weight_smem, wave_ref, rows_ref, synth_ref, analysis_ref, traj_ref, out_ref, wide, narrow):
    space = lax.axis_index("space")
    flip = space >= SPACE // 2
    first_weight = jnp.where(flip, SPACE - 1 - space, space) * LATS

    def widen(n, _):
        at = pl.ds(pl.multiple_of(n * (SLOTS * PART), SLOTS * PART), SLOTS * PART)
        wide[at, :] = rows_ref[n].astype(F32).reshape(SLOTS * PART, COLS)
        return 0

    lax.fori_loop(0, SPACE, widen, 0)
    wave = wave_ref[...]
    low = iota((M, COLS), 1) < ROWS

    def group(g, _):
        values_in, slopes_in = [], []
        for pair in range(GROUP // 2):
            t = g * GROUP + 2 * pair
            one = wide[pl.ds(t, M, stride=PART), :]
            two = wide[pl.ds(t + 1, M, stride=PART), :]
            real = jnp.where(low, one, pltpu.roll(two, ROWS, 1))
            imag = jnp.where(low, pltpu.roll(one, ROWS, 1), two)
            values_in.append(jnp.concatenate([real, imag], axis=0).astype(BF16))
            slopes_in.append(jnp.concatenate([-wave * imag, wave * real], axis=0).astype(BF16))
        values = dot(jnp.concatenate(values_in, axis=1), synth_ref[...], ((0,), (0,)))
        slopes = dot(jnp.concatenate(slopes_in, axis=1), synth_ref[...], ((0,), (0,)))
        pieces = []
        for q in range(GROUP):
            i = jnp.minimum(half * PART + g * GROUP + q, LATS - 1)
            t = jnp.where(flip, LATS - 1 - i, i)
            now = traj_ref[:, t].astype(F32)
            wind = jnp.concatenate([now[:, 0], now[:, 0]], axis=1)
            state = jnp.concatenate([now[:, 2], now[:, 1]], axis=1)
            v = values[q * ROWS : (q + 1) * ROWS].reshape(8, 8, NLON)
            s = slopes[q * ROWS : (q + 1) * ROWS].reshape(8, 8, NLON)
            forcing = (wind * s + state * v) * -weight_smem[first_weight + i]
            pieces.append(forcing.reshape(ROWS, NLON).astype(BF16))
        forcing = jnp.concatenate(pieces, axis=0)
        waves = dot(analysis_ref[...], forcing, ((1,), (1,)))
        for pair in range(GROUP // 2):
            t = g * GROUP + 2 * pair
            real = waves[0:M, pair * COLS : (pair + 1) * COLS]
            imag = waves[M : 2 * M, pair * COLS : (pair + 1) * COLS]
            narrow[pl.ds(t, M, stride=PART), :] = jnp.where(low, real, pltpu.roll(imag, ROWS, 1))
            narrow[pl.ds(t + 1, M, stride=PART), :] = jnp.where(low, pltpu.roll(real, ROWS, 1), imag)
        return 0

    lax.fori_loop(0, PART // GROUP, group, 0)

    def shrink(n, _):
        at = pl.ds(pl.multiple_of(n * (SLOTS * PART), SLOTS * PART), SLOTS * PART)
        out_ref[n] = narrow[at, :].reshape(SLOTS, PART, COLS).astype(BF16)
        return 0

    lax.fori_loop(0, SPACE, shrink, 0)


def remote(src, dst, send, recv, **to):
    return pltpu.make_async_remote_copy(
        src, dst, send, recv, device_id=to, device_id_type=MESH
    )


def steps_kernel(
    wave_smem, weight_smem, wave_ref, table_ref, state_ref, mix_ref, speed_ref, first_ref, own_ref, part_ref,
    out_ref,
    traj, synth, analysis, there_0, there_1, grid_0, grid_1, back_0, back_1, second, middle, wide, narrow,
    send_sem, recv_sem, own_sem, ring_send, ring_recv, ring_own,
):
    me = lax.axis_index("space")
    pert = lax.axis_index("pert")
    side, y = pert // 4, lax.rem(pert, 4)
    after, before = side * 4 + lax.rem(y + 1, 4), side * 4 + lax.rem(y + 3, 4)
    barrier = pltpu.get_barrier_semaphore()

    def greet(i, _):
        pl.semaphore_signal(
            barrier, inc=1, device_id={"space": lax.rem(me + i, SPACE)}, device_id_type=MESH
        )
        return 0

    lax.fori_loop(1, SPACE, greet, 0)
    for neighbour in (after, before):
        pl.semaphore_signal(barrier, inc=1, device_id={"pert": neighbour}, device_id_type=MESH)
    pl.semaphore_wait(barrier, SPACE + 1)

    exchanges = ((first_ref, there_0), (grid_0, back_0), (second, there_1), (grid_1, back_1))

    def own_copy(e, chunk, half, slots):
        src, dst = exchanges[e]
        return pltpu.make_async_copy(
            src.at[half, me, slots], dst.at[half, me, slots], own_sem.at[e, chunk]
        )

    def push(e, chunk, half, slots=pl.ds(0, SLOTS)):
        src, dst = exchanges[e]

        def start(i, _):
            to = lax.rem(me + i, SPACE)
            remote(
                src.at[half, to, slots], dst.at[half, me, slots],
                send_sem.at[e, chunk], recv_sem.at[e, chunk], space=to,
            ).start()
            return 0

        lax.fori_loop(1, SPACE, start, 0)
        own_copy(e, chunk, half, slots).start()

    def everyone(e, chunk, half, slots):
        src, dst = exchanges[e]
        others = pl.ds(0, SPACE - 1)
        return remote(
            src.at[half, others, slots], dst.at[half, others, slots],
            send_sem.at[e, chunk], recv_sem.at[e, chunk], space=lax.rem(me + 1, SPACE),
        )

    def arrive(e, chunk, half, slots=pl.ds(0, SLOTS)):
        everyone(e, chunk, half, slots).wait_recv()
        own_copy(e, chunk, half, slots).wait()

    def drain(e, chunk, half, slots=pl.ds(0, SLOTS)):
        everyone(e, chunk, half, slots).wait_send()

    for half in range(2):
        push(0, half, half)
    rings, locals_ = [], []
    for step in range(STEPS):
        for n, (block, group) in enumerate(
            ((own_ref.at[step], side * 4), (part_ref.at[step], (1 - side) * 4))
        ):
            here = traj.at[step, group + y]
            locals_.append(pltpu.make_async_copy(block, here, ring_own.at[step, n]))
            for way, to in enumerate((after, before)):
                at = 2 * n + way
                rings.append(remote(block, here, ring_send.at[step, at], ring_recv.at[step, at], pert=to))
    for c in rings + locals_:
        c.start()
    passed = []

    def pass_on(step):
        cut = LATS // 2 + 1
        for n, group in enumerate((side * 4, (1 - side) * 4)):
            for way, (origin, rows, to) in enumerate((
                (group + lax.rem(y + 3, 4), pl.ds(0, cut), after),
                (group + lax.rem(y + 1, 4), pl.ds(cut, LATS - cut), before),
            )):
                rings[4 * step + 2 * n + way].wait_recv()
                piece = traj.at[step, origin, rows]
                at = 4 + 2 * n + way
                passed.append(
                    remote(piece, piece, ring_send.at[step, at], ring_recv.at[step, at], pert=to)
                )
                passed[-1].start()

    zonal_tables(wave_ref, synth, analysis)
    pass_on(0)
    speed = speed_ref[0:1, :]
    base = me * SLOTS

    new, old = iota((2 * COLS, COLS), 0), iota((2 * COLS, COLS), 1)
    perm = reordered(old, new % COLS).astype(BF16)

    def slot(step, j):
        w = wave_smem[base + j]
        if step == 0:
            result = updated(j, w, table_ref, state_ref, back_0, mix_ref, speed)
            middle[j] = result
            legendre_rows(j, table_ref, result.astype(BF16), second)
        else:
            result = updated(j, w, table_ref, middle, back_1, mix_ref, speed)
            result = dot(split(result), perm)
            for parity in range(2):
                out_ref[j, pl.ds(parity, HK, stride=2), :] = result[parity * HK : (parity + 1) * HK]

    few = SLOTS // 2
    early, late = pl.ds(0, few), pl.ds(few, few)
    for step in range(STEPS):
        rows, out = (there_0, grid_0) if step == 0 else (there_1, grid_1)
        back = 2 * step + 1
        for half in range(2):
            if step == 0:
                arrive(0, half, half)
            else:
                arrive(2, half, half, early)
                arrive(2, 2 + half, half, late)
            if half == 0:
                for c in passed[4 * step :]:
                    c.wait_recv()
                for c in locals_[2 * step : 2 * step + 2]:
                    c.wait()
            grid_half(
                half, weight_smem, wave_ref, rows.at[half], synth, analysis, traj.at[step], out.at[half], wide, narrow
            )
            if half == 0:
                push(back, 0, 0)
            else:
                push(back, 1, 1, early)
                push(back, 2, 1, late)
        if step == 0:
            pass_on(1)
        arrive(back, 0, 0)
        arrive(back, 1, 1, early)
        for j in range(few):
            slot(step, j)
        if step == 0:
            push(2, 0, 0, early)
        arrive(back, 2, 1, late)
        for j in range(few, SLOTS):
            slot(step, j)
        if step == 0:
            push(2, 2, 0, late)
            push(2, 1, 1, early)
            push(2, 3, 1, late)
    for half in range(2):
        drain(0, half, half)
        drain(2, half, half, early)
        drain(2, 2 + half, half, late)
    for e in (1, 3):
        drain(e, 0, 0)
        drain(e, 1, 1, early)
        drain(e, 2, 1, late)
    for c in rings + passed:
        c.wait_send()


VMEM = pl.BlockSpec(memory_space=pltpu.VMEM)
SMEM = pl.BlockSpec(memory_space=pltpu.SMEM)
ANY = pl.BlockSpec(memory_space=pl.ANY)
PARAMS = pltpu.CompilerParams(vmem_limit_bytes=60 * 2**20)


def shards(spectra, wave_order, traj_wind, traj_state, vertical_modes, mode_speeds):
    lat_rows, weight = northern()
    fields = jnp.concatenate([traj_wind[:, None], traj_state], axis=1)
    fields = jnp.transpose(fields, (0, 3, 1, 2, 4))
    partner = lax.ppermute(fields, "pert", [(p, (p + 4) % PERT) for p in range(PERT)])
    wave_rows = wave_order.astype(F32)[:, None]

    rows_shape = (2, SPACE, SLOTS, PART, COLS)
    send_shape = jax.ShapeDtypeStruct(rows_shape, BF16)
    state_shape = jax.ShapeDtypeStruct((SLOTS, M, COLS), F32)
    table, state, send, mix, speed = pl.pallas_call(
        table_kernel,
        out_shape=(
            jax.ShapeDtypeStruct((SLOTS, M, HALF), BF16),
            state_shape,
            send_shape,
            jax.ShapeDtypeStruct((2, 2 * COLS, 2 * COLS), BF16),
            jax.ShapeDtypeStruct((8, COLS), F32),
        ),
        in_specs=[SMEM] + [VMEM] * 4,
        out_specs=(VMEM,) * 5,
        scratch_shapes=[pltpu.VMEM((2, 16 * M, 128), F32), pltpu.VMEM((2, 3, 16, 128), F32)],
        compiler_params=PARAMS,
        cost_estimate=pl.CostEstimate(flops=10**10, bytes_accessed=3 * 10**7, transcendentals=10**6),
        name="table_stage",
    )(wave_order, jnp.asarray(lat_rows), spectra, vertical_modes, mode_speeds[None])
    return pl.pallas_call(
        steps_kernel,
        out_shape=state_shape,
        in_specs=[SMEM] * 2 + [VMEM] * 5 + [ANY] * 3,
        out_specs=VMEM,
        scratch_shapes=[
            pltpu.VMEM((STEPS, PERT, LATS, 3, 4, NLON), BF16),
            pltpu.VMEM((2 * M, NLON), BF16),
            pltpu.VMEM((2 * M, NLON), BF16),
        ]
        + [pltpu.VMEM(rows_shape, BF16)] * 7
        + [pltpu.VMEM((SLOTS, M, COLS), F32)]
        + [pltpu.VMEM((M * PART, COLS), F32)] * 2
        + [pltpu.SemaphoreType.DMA((4, 4))] * 3
        + [pltpu.SemaphoreType.DMA((STEPS, 8))] * 2
        + [pltpu.SemaphoreType.DMA((STEPS, 2))],
        compiler_params=pltpu.CompilerParams(
            collective_id=1, has_side_effects=True, vmem_limit_bytes=60 * 2**20
        ),
        name="steps",
    )(wave_order, jnp.asarray(weight), wave_rows, table, state, mix, speed, send, fields, partner)


def solution(mesh):
    placed = (
        P("space", None, "pert"),
        P(),
        P(None, "pert", "space", None),
        P(None, None, "pert", "space", None),
        P(),
        P(),
    )
    return jax.shard_map(
        shards, mesh=mesh, in_specs=placed, out_specs=P("space", None, "pert"), check_vma=False
    )
```

```python
import math

import jax
import jax.numpy as jnp
import numpy as np
from jax import lax
from jax.experimental import pallas as pl
from jax.experimental.pallas import tpu as pltpu
from jax.sharding import PartitionSpec as P

NLAT = 480
NLON = 960
M = 320
VARS = 2
LEV = 32
STEPS = 2
PERT = 8
SPACE = 32
SLOTS = M // SPACE
LATS = NLAT // SPACE
PAD = 16
HALF = (SPACE // 2) * PAD
COLS = 128
ROWS = COLS // 2
HK = M // 2
APART = M + 8
PART = PAD // 2
CHUNKS = 8
GROUP = 4
F32 = jnp.float32
BF16 = jnp.bfloat16
MESH = pl.DeviceIdType.MESH
HIGHEST = lax.Precision.HIGHEST


def dot(a, b, dims=((1,), (0,)), precision=None):
    return lax.dot_general(
        a, b, (dims, ((), ())), preferred_element_type=F32, precision=precision
    )


def iota(shape, axis):
    return lax.broadcasted_iota(jnp.int32, shape, axis)


def level_of(new):
    return new % ROWS // 8 * 4 + new % 4


def group_of(new):
    return new // ROWS * 2 + new % 8 // 4


def reordered(old, new):
    return old == new % 8 // 4 * 64 + level_of(new) * 2 + new // ROWS


def split(x):
    high = x.astype(BF16)
    return jnp.concatenate([high, (x - high.astype(F32)).astype(BF16)], axis=1)


def northern():
    place = np.arange(HALF)
    row = place // COLS * PART + place % PART
    inside = row < LATS
    lat = np.minimum(place % COLS // PART * LATS + row, NLAT // 2 - 1)
    angle = (lat + 0.5) * (math.pi / NLAT)
    rows = np.stack([np.cos(angle), np.log(np.sin(angle)), inside.astype(np.float64)])
    weight = np.sin((np.arange(NLAT // 2) + 0.5) * (math.pi / NLAT)) * (math.pi / NLAT)
    return rows.astype(np.float32), weight.astype(np.float32)


def keep_of(w):
    row = iota((M, COLS), 0)
    degree = jnp.where(row < HK, 2 * row, 2 * row - (M - 1)) + w
    keep = (degree <= M - 1) & jnp.logical_not((iota((M, COLS), 1) >= ROWS) & (w == 0))
    return keep.astype(F32), degree


def legendre_rows(j, table_ref, state, send_ref):
    even, odd = state[:HK], state[HK:]
    both = jnp.concatenate(
        [jnp.concatenate([even, even], axis=1), jnp.concatenate([odd, -odd], axis=1)], axis=0
    )
    rows = dot(table_ref[j], both, ((0,), (0,)))
    for half in range(2):
        for d in range(SPACE // 2):
            at = half * COLS + d * PART
            send_ref[half, d, j] = rows[at : at + PART, :COLS].astype(BF16)
            send_ref[half, SPACE - 1 - d, j] = rows[at : at + PART, COLS:].astype(BF16)


def implicit_operators(modes_ref, speeds_ref, mix_ref, speed_ref):
    lev = iota((LEV, COLS), 0)
    onehot = (level_of(iota((LEV, COLS), 1)) == lev).astype(F32)
    same = (group_of(iota((COLS, COLS), 0)) == group_of(iota((COLS, COLS), 1))).astype(F32)
    for way in range(2):
        spread = dot(onehot, modes_ref[...], ((0,), (1 - way,)), HIGHEST)
        mix = dot(spread, onehot, precision=HIGHEST) * same
        high = mix.astype(BF16)
        low = (mix - high.astype(F32)).astype(BF16)
        mix_ref[way, :COLS, :COLS] = high
        mix_ref[way, :COLS, COLS:] = low
        mix_ref[way, COLS:, :COLS] = high
        mix_ref[way, COLS:, COLS:] = jnp.zeros_like(low)
    speed_ref[...] = dot(jnp.broadcast_to(speeds_ref[...], (8, LEV)), onehot, precision=HIGHEST)


def recurrence(wave_smem, lat_ref, scratch, coefs, between):
    base = lax.axis_index("space") * SLOTS
    row16 = iota((16, 128), 0)
    wave = jnp.zeros((16, 128), jnp.int32)
    for j in range(SLOTS):
        wave = jnp.where(row16 == j, wave_smem[base + j], wave)
    wave = wave.astype(F32)
    cosines = [lat_ref[0:1, c * 128 : (c + 1) * 128] for c in range(2)]
    number = (iota((16, 384), 1) + 1).astype(F32)
    terms = jnp.where(number <= wave[:, 0:1], jnp.log((2.0 * number + 1.0) / (2.0 * number)), 0.0)
    start = 0.5 * jnp.sum(terms, axis=1, keepdims=True) - 0.5 * math.log(2.0)
    starts = [start + wave * lat_ref[1:2, c * 128 : (c + 1) * 128] for c in range(2)]
    inside = [lat_ref[2:3, c * 128 : (c + 1) * 128] for c in range(2)]

    def coefficient(up, w):
        return jnp.sqrt((4.0 * (w + up) * (w + up) - 1.0) / (up * (2.0 * w + up)))

    for c in range(3):
        up = (iota((16, 128), 1) + (c * 128 + 1)).astype(F32)
        coefs[0, c] = coefficient(up, wave)
        coefs[1, c] = coefs[0, c] / coefficient(jnp.maximum(up - 1.0, 1.0), wave)

    def block(b, carry):
        current, previous, logs = (list(x) for x in carry)
        factor = [jnp.exp(starts[c] + logs[c]) * inside[c] for c in range(2)]
        shift = lax.rem(128 - 16 * lax.rem(b, 8), 128)
        coef, ratio = (pltpu.roll(coefs[n, b // 8], shift, 1) for n in range(2))
        for i in range(16):
            row = (i % 2) * HK + b * 8 + i // 2
            up, down = (jnp.broadcast_to(x[:, i : i + 1], (16, 128)) for x in (coef, ratio))
            for c in range(2):
                scratch[c, pl.ds(row, 16, stride=APART), :] = current[c] * factor[c]
                following = (up * cosines[c]) * current[c] - down * previous[c]
                previous[c] = current[c]
                current[c] = following
        for c in range(2):
            biggest = jnp.maximum(jnp.abs(current[c]), jnp.abs(previous[c]))
            shrink = 1.0 / biggest
            current[c] = current[c] * shrink
            previous[c] = previous[c] * shrink
            logs[c] = logs[c] + jnp.log(biggest)
        return tuple(current), tuple(previous), tuple(logs)

    ones = jnp.ones((16, 128), F32)
    zeros = jnp.zeros((16, 128), F32)
    half_way = lax.fori_loop(0, M // 32, block, ((ones, ones), (zeros, zeros), (zeros, zeros)))
    between()
    lax.fori_loop(M // 32, M // 16, block, half_way)


def first_rows(j, w, spectra_ref, scratch, table_ref, state_ref, send_ref):
    old, new = iota((2 * COLS, 2 * COLS), 0), iota((2 * COLS, 2 * COLS), 1)
    perm = (reordered(old % COLS, new % COLS) & (old // COLS == new // COLS)).astype(BF16)
    for c in range(2):
        table_ref[j, :, c * 128 : (c + 1) * 128] = scratch[c, pl.ds(j * APART, M), :].astype(BF16)
    keep, _ = keep_of(w)
    given = jnp.concatenate(
        [spectra_ref[j, pl.ds(parity, HK, stride=2), :] for parity in range(2)], axis=0
    )
    moved = dot(split(given), perm)
    high = moved[:, :COLS] * keep
    state_ref[j] = high + moved[:, COLS:] * keep
    legendre_rows(j, table_ref, high.astype(BF16), send_ref)


def updated(j, w, table_ref, state_ref, rows_ref, mix_ref, speed):
    sides = []
    for order in (lambda d: d, lambda d: SPACE - 1 - d):
        pieces = [
            rows_ref[half, order(d), j].astype(F32) for half in range(2) for d in range(SPACE // 2)
        ]
        sides.append(jnp.concatenate(pieces, axis=0).astype(BF16))
    change = dot(table_ref[j], jnp.concatenate(sides, axis=1))
    north, south = change[:, :COLS], change[:, COLS:]
    change = jnp.concatenate([north[:HK] + south[:HK], north[HK:] - south[HK:]], axis=0)
    combined = state_ref[j] + change
    keep, degree = keep_of(w)
    stiffness = speed * (degree * (degree + 1)).astype(F32)
    damping = stiffness / (1.0 + stiffness)
    projected = dot(split(combined), mix_ref[0])
    projected = damping * (projected[:, :COLS] + projected[:, COLS:])
    returned = dot(split(projected), mix_ref[1])
    return (combined - (returned[:, :COLS] + returned[:, COLS:])) * keep


def zonal_tables(wave_ref, synth_ref, analysis_ref):
    step = 2.0 * math.pi / NLON

    def angle_of(count):
        return (count - NLON * jnp.floor(count * (1.0 / NLON))) * step

    def rows(i, _):
        at = pl.ds(pl.multiple_of(i * 64, 64), 64)
        below = pl.ds(pl.multiple_of(M + i * 64, 64), 64)
        wave = wave_ref[at, :].astype(F32)
        x = iota((64, 128), 1).astype(F32)
        angle = angle_of(wave * x)
        turn = angle_of(wave * jnp.full((64, 128), 128.0, F32))
        cosine, sine = jnp.cos(angle), jnp.sin(angle)
        turn_cosine, turn_sine = jnp.cos(turn), jnp.sin(turn)
        factor = jnp.where(wave == 0.0, 1.0, 2.0)
        for c in range(CHUNKS):
            width = min(128, NLON - c * 128)
            lanes = slice(c * 128, c * 128 + width)
            synth_ref[at, lanes] = (factor * cosine)[:, :width].astype(BF16)
            synth_ref[below, lanes] = (-factor * sine)[:, :width].astype(BF16)
            analysis_ref[at, lanes] = (cosine * (1.0 / NLON))[:, :width].astype(BF16)
            analysis_ref[below, lanes] = (sine * (-1.0 / NLON))[:, :width].astype(BF16)
            cosine, sine = (
                cosine * turn_cosine - sine * turn_sine,
                sine * turn_cosine + cosine * turn_sine,
            )
        return 0

    lax.fori_loop(0, M // 64, rows, 0)


def grid_half(half, weight_smem, wave_ref, rows_ref, synth_ref, analysis_ref, traj_ref, out_ref, wide, narrow):
    space = lax.axis_index("space")
    flip = space >= SPACE // 2
    first_weight = jnp.where(flip, SPACE - 1 - space, space) * LATS

    def widen(n, _):
        at = pl.ds(pl.multiple_of(n * (SLOTS * PART), SLOTS * PART), SLOTS * PART)
        wide[at, :] = rows_ref[n].astype(F32).reshape(SLOTS * PART, COLS)
        return 0

    lax.fori_loop(0, SPACE, widen, 0)
    wave = wave_ref[...].astype(F32)
    low = iota((M, COLS), 1) < ROWS

    def group(g, _):
        values_in, slopes_in = [], []
        for pair in range(GROUP // 2):
            t = g * GROUP + 2 * pair
            one = wide[pl.ds(t, M, stride=PART), :]
            two = wide[pl.ds(t + 1, M, stride=PART), :]
            real = jnp.where(low, one, pltpu.roll(two, ROWS, 1))
            imag = jnp.where(low, pltpu.roll(one, ROWS, 1), two)
            values_in.append(jnp.concatenate([real, imag], axis=0).astype(BF16))
            slopes_in.append(jnp.concatenate([-wave * imag, wave * real], axis=0).astype(BF16))
        values = dot(jnp.concatenate(values_in, axis=1), synth_ref[...], ((0,), (0,)))
        slopes = dot(jnp.concatenate(slopes_in, axis=1), synth_ref[...], ((0,), (0,)))
        pieces = []
        for q in range(GROUP):
            i = jnp.minimum(half * PART + g * GROUP + q, LATS - 1)
            t = jnp.where(flip, LATS - 1 - i, i)
            now = traj_ref[:, t].astype(F32)
            wind = jnp.concatenate([now[:, 0], now[:, 0]], axis=1)
            state = jnp.concatenate([now[:, 2], now[:, 1]], axis=1)
            v = values[q * ROWS : (q + 1) * ROWS].reshape(8, 8, NLON)
            s = slopes[q * ROWS : (q + 1) * ROWS].reshape(8, 8, NLON)
            forcing = (wind * s + state * v) * -weight_smem[first_weight + i]
            pieces.append(forcing.reshape(ROWS, NLON).astype(BF16))
        forcing = jnp.concatenate(pieces, axis=0)
        waves = dot(analysis_ref[...], forcing, ((1,), (1,)))
        for pair in range(GROUP // 2):
            t = g * GROUP + 2 * pair
            real = waves[0:M, pair * COLS : (pair + 1) * COLS]
            imag = waves[M : 2 * M, pair * COLS : (pair + 1) * COLS]
            narrow[pl.ds(t, M, stride=PART), :] = jnp.where(low, real, pltpu.roll(imag, ROWS, 1))
            narrow[pl.ds(t + 1, M, stride=PART), :] = jnp.where(low, pltpu.roll(real, ROWS, 1), imag)
        return 0

    lax.fori_loop(0, PART // GROUP, group, 0)

    def shrink(n, _):
        at = pl.ds(pl.multiple_of(n * (SLOTS * PART), SLOTS * PART), SLOTS * PART)
        out_ref[n] = narrow[at, :].reshape(SLOTS, PART, COLS).astype(BF16)
        return 0

    lax.fori_loop(0, SPACE, shrink, 0)


def remote(src, dst, send, recv, **to):
    return pltpu.make_async_remote_copy(
        src, dst, send, recv, device_id=to, device_id_type=MESH
    )


def steps_kernel(
    wave_smem, weight_smem, wave_ref, lat_ref, spectra_ref, modes_ref, speeds_ref, own_ref,
    out_ref,
    part, scratch, coefs, table_ref, state_ref, mix_ref, speed_ref, first_ref,
    traj, synth, analysis, there_0, there_1, grid_0, grid_1, back_0, back_1, second, middle, wide, narrow,
    send_sem, recv_sem, own_sem, ring_send, ring_recv, ring_own, part_send, part_recv,
):
    me = lax.axis_index("space")
    pert = lax.axis_index("pert")
    side, y = pert // 4, lax.rem(pert, 4)
    after, before = side * 4 + lax.rem(y + 1, 4), side * 4 + lax.rem(y + 3, 4)
    barrier = pltpu.get_barrier_semaphore()

    def greet(i, _):
        pl.semaphore_signal(
            barrier, inc=1, device_id={"space": lax.rem(me + i, SPACE)}, device_id_type=MESH
        )
        return 0

    lax.fori_loop(1, SPACE, greet, 0)
    partner = lax.rem(pert + 4, PERT)
    for neighbour in (after, before, partner):
        pl.semaphore_signal(barrier, inc=1, device_id={"pert": neighbour}, device_id_type=MESH)

    exchanges = ((first_ref, there_0), (grid_0, back_0), (second, there_1), (grid_1, back_1))

    def own_copy(e, chunk, half, slots):
        src, dst = exchanges[e]
        return pltpu.make_async_copy(
            src.at[half, me, slots], dst.at[half, me, slots], own_sem.at[e, chunk]
        )

    def push(e, chunk, half, slots=pl.ds(0, SLOTS)):
        src, dst = exchanges[e]

        def start(i, _):
            to = lax.rem(me + i, SPACE)
            remote(
                src.at[half, to, slots], dst.at[half, me, slots],
                send_sem.at[e, chunk], recv_sem.at[e, chunk], space=to,
            ).start()
            return 0

        lax.fori_loop(1, SPACE, start, 0)
        own_copy(e, chunk, half, slots).start()

    def everyone(e, chunk, half, slots):
        src, dst = exchanges[e]
        others = pl.ds(0, SPACE - 1)
        return remote(
            src.at[half, others, slots], dst.at[half, others, slots],
            send_sem.at[e, chunk], recv_sem.at[e, chunk], space=lax.rem(me + 1, SPACE),
        )

    def arrive(e, chunk, half, slots=pl.ds(0, SLOTS)):
        everyone(e, chunk, half, slots).wait_recv()
        own_copy(e, chunk, half, slots).wait()

    def drain(e, chunk, half, slots=pl.ds(0, SLOTS)):
        everyone(e, chunk, half, slots).wait_send()

    crossing = [
        remote(own_ref.at[step], part.at[step], part_send.at[step], part_recv.at[step], pert=partner)
        for step in range(STEPS)
    ]
    rings, locals_ = {}, {}
    for step in range(STEPS):
        for n, (block, group) in enumerate(
            ((own_ref.at[step], side * 4), (part.at[step], (1 - side) * 4))
        ):
            here = traj.at[step, group + y]
            locals_[step, n] = pltpu.make_async_copy(block, here, ring_own.at[step, n])
            for way, to in enumerate((after, before)):
                at = 2 * n + way
                rings[step, at] = remote(
                    block, here, ring_send.at[step, at], ring_recv.at[step, at], pert=to
                )

    def send_round(step, n):
        locals_[step, n].start()
        for way in range(2):
            rings[step, 2 * n + way].start()

    def between():
        pl.semaphore_wait(barrier, SPACE + 2)
        for step in range(STEPS):
            crossing[step].start()
        for step in range(STEPS):
            send_round(step, 0)

    recurrence(wave_smem, lat_ref, scratch, coefs, between)
    base = me * SLOTS
    few = SLOTS // 2
    early, late = pl.ds(0, few), pl.ds(few, few)
    for j in range(SLOTS):
        first_rows(j, wave_smem[base + j], spectra_ref, scratch, table_ref, state_ref, first_ref)
        if j == few - 1:
            push(0, 0, 0, early)
    push(0, 2, 0, late)
    push(0, 1, 1, early)
    push(0, 3, 1, late)
    crossing[0].wait_recv()
    send_round(0, 1)
    implicit_operators(modes_ref, speeds_ref, mix_ref, speed_ref)
    passed = []

    def pass_on(step):
        cut = LATS // 2 + 1
        for n, group in enumerate((side * 4, (1 - side) * 4)):
            for way, (origin, rows, to) in enumerate((
                (group + lax.rem(y + 3, 4), pl.ds(0, cut), after),
                (group + lax.rem(y + 1, 4), pl.ds(cut, LATS - cut), before),
            )):
                rings[step, 2 * n + way].wait_recv()
                piece = traj.at[step, origin, rows]
                at = 4 + 2 * n + way
                passed.append(
                    remote(piece, piece, ring_send.at[step, at], ring_recv.at[step, at], pert=to)
                )
                passed[-1].start()

    zonal_tables(wave_ref, synth, analysis)
    crossing[1].wait_recv()
    send_round(1, 1)
    pass_on(0)
    speed = speed_ref[0:1, :]

    new, old = iota((2 * COLS, COLS), 0), iota((2 * COLS, COLS), 1)
    perm = reordered(old, new % COLS).astype(BF16)

    def slot(step, j):
        w = wave_smem[base + j]
        if step == 0:
            result = updated(j, w, table_ref, state_ref, back_0, mix_ref, speed)
            middle[j] = result
            legendre_rows(j, table_ref, result.astype(BF16), second)
        else:
            result = updated(j, w, table_ref, middle, back_1, mix_ref, speed)
            result = dot(split(result), perm)
            for parity in range(2):
                out_ref[j, pl.ds(parity, HK, stride=2), :] = result[parity * HK : (parity + 1) * HK]

    for step in range(STEPS):
        rows, out = (there_0, grid_0) if step == 0 else (there_1, grid_1)
        back = 2 * step + 1
        for half in range(2):
            arrive(2 * step, half, half, early)
            arrive(2 * step, 2 + half, half, late)
            if half == 0:
                for c in passed[4 * step :]:
                    c.wait_recv()
                for n in range(2):
                    locals_[step, n].wait()
            grid_half(
                half, weight_smem, wave_ref, rows.at[half], synth, analysis, traj.at[step], out.at[half], wide, narrow
            )
            if half == 0:
                push(back, 0, 0)
            else:
                push(back, 1, 1, early)
                push(back, 2, 1, late)
        if step == 0:
            pass_on(1)
        arrive(back, 0, 0)
        arrive(back, 1, 1, early)
        for j in range(few):
            slot(step, j)
        if step == 0:
            push(2, 0, 0, early)
        arrive(back, 2, 1, late)
        for j in range(few, SLOTS):
            slot(step, j)
        if step == 0:
            push(2, 2, 0, late)
            push(2, 1, 1, early)
            push(2, 3, 1, late)
    for e in (0, 2):
        for half in range(2):
            drain(e, half, half, early)
            drain(e, 2 + half, half, late)
    for e in (1, 3):
        drain(e, 0, 0)
        drain(e, 1, 1, early)
        drain(e, 2, 1, late)
    for c in list(rings.values()) + passed + crossing:
        c.wait_send()


VMEM = pl.BlockSpec(memory_space=pltpu.VMEM)
SMEM = pl.BlockSpec(memory_space=pltpu.SMEM)
ANY = pl.BlockSpec(memory_space=pl.ANY)


def shards(spectra, wave_order, traj_wind, traj_state, vertical_modes, mode_speeds):
    lat_rows, weight = northern()
    fields = jnp.concatenate([traj_wind[:, None], traj_state], axis=1)
    fields = jnp.transpose(fields, (0, 3, 1, 2, 4))
    rows_shape = (2, SPACE, SLOTS, PART, COLS)
    return pl.pallas_call(
        steps_kernel,
        out_shape=jax.ShapeDtypeStruct((SLOTS, M, COLS), F32),
        in_specs=[SMEM] * 2 + [VMEM] * 5 + [ANY],
        out_specs=VMEM,
        scratch_shapes=[
            pltpu.VMEM(fields.shape, BF16),
            pltpu.VMEM((2, 16 * APART, 128), F32),
            pltpu.VMEM((2, 3, 16, 128), F32),
            pltpu.VMEM((SLOTS, M, HALF), BF16),
            pltpu.VMEM((SLOTS, M, COLS), F32),
            pltpu.VMEM((2, 2 * COLS, 2 * COLS), BF16),
            pltpu.VMEM((8, COLS), F32),
            pltpu.VMEM(rows_shape, BF16),
            pltpu.VMEM((STEPS, PERT, LATS, 3, 4, NLON), BF16),
            pltpu.VMEM((2 * M, NLON), BF16),
            pltpu.VMEM((2 * M, NLON), BF16),
        ]
        + [pltpu.VMEM(rows_shape, BF16)] * 7
        + [pltpu.VMEM((SLOTS, M, COLS), F32)]
        + [pltpu.VMEM((M * PART, COLS), F32)] * 2
        + [pltpu.SemaphoreType.DMA((4, 4))] * 3
        + [pltpu.SemaphoreType.DMA((STEPS, 8))] * 2
        + [pltpu.SemaphoreType.DMA((STEPS, 2))]
        + [pltpu.SemaphoreType.DMA((STEPS,))] * 2,
        compiler_params=pltpu.CompilerParams(
            collective_id=1, has_side_effects=True, vmem_limit_bytes=60 * 2**20
        ),
        name="steps",
    )(
        wave_order, jnp.asarray(weight), wave_order[:, None], jnp.asarray(lat_rows), spectra,
        vertical_modes, mode_speeds[None], fields,
    )


def solution(mesh):
    placed = (
        P("space", None, "pert"),
        P(),
        P(None, "pert", "space", None),
        P(None, None, "pert", "space", None),
        P(),
        P(),
    )
    return jax.shard_map(
        shards, mesh=mesh, in_specs=placed, out_specs=P("space", None, "pert"), check_vma=False
    )
```

```python
import math

import jax
import jax.numpy as jnp
import numpy as np
from jax import lax
from jax.experimental import pallas as pl
from jax.experimental.pallas import tpu as pltpu
from jax.sharding import PartitionSpec as P

NLAT = 480
NLON = 960
M = 320
VARS = 2
LEV = 32
STEPS = 2
PERT = 8
SPACE = 32
SLOTS = M // SPACE
LATS = NLAT // SPACE
PAD = 16
HALF = (SPACE // 2) * PAD
COLS = 128
ROWS = COLS // 2
HK = M // 2
APART = M + 8
PART = PAD // 2
CHUNKS = 8
GROUP = 4
F32 = jnp.float32
BF16 = jnp.bfloat16
MESH = pl.DeviceIdType.MESH
HIGHEST = lax.Precision.HIGHEST


def dot(a, b, dims=((1,), (0,)), precision=None):
    return lax.dot_general(
        a, b, (dims, ((), ())), preferred_element_type=F32, precision=precision
    )


def iota(shape, axis):
    return lax.broadcasted_iota(jnp.int32, shape, axis)


def level_of(new):
    return new % ROWS // 8 * 4 + new % 4


def group_of(new):
    return new // ROWS * 2 + new % 8 // 4


def reordered(old, new):
    return old == new % 8 // 4 * 64 + level_of(new) * 2 + new // ROWS


def split(x):
    high = x.astype(BF16)
    return jnp.concatenate([high, (x - high.astype(F32)).astype(BF16)], axis=1)


def northern():
    place = np.arange(HALF)
    row = place // COLS * PART + place % PART
    inside = row < LATS
    lat = np.minimum(place % COLS // PART * LATS + row, NLAT // 2 - 1)
    angle = (lat + 0.5) * (math.pi / NLAT)
    rows = np.stack([np.cos(angle), np.log(np.sin(angle)), inside.astype(np.float64)])
    weight = np.sin((np.arange(NLAT // 2) + 0.5) * (math.pi / NLAT)) * (math.pi / NLAT)
    return rows.astype(np.float32), weight.astype(np.float32)


def keep_of(w):
    row = iota((M, COLS), 0)
    degree = jnp.where(row < HK, 2 * row, 2 * row - (M - 1)) + w
    keep = (degree <= M - 1) & jnp.logical_not((iota((M, COLS), 1) >= ROWS) & (w == 0))
    return keep.astype(F32), degree


def legendre_rows(j, table_ref, state, send_ref):
    even, odd = state[:HK], state[HK:]
    both = jnp.concatenate(
        [jnp.concatenate([even, even], axis=1), jnp.concatenate([odd, -odd], axis=1)], axis=0
    )
    rows = dot(table_ref[j], both, ((0,), (0,)))
    for half in range(2):
        for d in range(SPACE // 2):
            at = half * COLS + d * PART
            send_ref[half, d, j] = rows[at : at + PART, :COLS].astype(BF16)
            send_ref[half, SPACE - 1 - d, j] = rows[at : at + PART, COLS:].astype(BF16)


def implicit_operators(modes_ref, speeds_ref, mix_ref, speed_ref):
    lev = iota((LEV, COLS), 0)
    onehot = (level_of(iota((LEV, COLS), 1)) == lev).astype(F32)
    same = (group_of(iota((COLS, COLS), 0)) == group_of(iota((COLS, COLS), 1))).astype(F32)
    for way in range(2):
        spread = dot(onehot, modes_ref[...], ((0,), (1 - way,)), HIGHEST)
        mix = dot(spread, onehot, precision=HIGHEST) * same
        high = mix.astype(BF16)
        low = (mix - high.astype(F32)).astype(BF16)
        mix_ref[way, :COLS, :COLS] = high
        mix_ref[way, :COLS, COLS:] = low
        mix_ref[way, COLS:, :COLS] = high
        mix_ref[way, COLS:, COLS:] = jnp.zeros_like(low)
    speed_ref[...] = dot(jnp.broadcast_to(speeds_ref[...], (8, LEV)), onehot, precision=HIGHEST)


def recurrence(wave_smem, lat_ref, scratch, coefs, between):
    base = lax.axis_index("space") * SLOTS
    row16 = iota((16, 128), 0)
    wave = jnp.zeros((16, 128), jnp.int32)
    for j in range(SLOTS):
        wave = jnp.where(row16 == j, wave_smem[base + j], wave)
    wave = wave.astype(F32)
    cosines = [lat_ref[0:1, c * 128 : (c + 1) * 128] for c in range(2)]
    number = (iota((16, 384), 1) + 1).astype(F32)
    terms = jnp.where(number <= wave[:, 0:1], jnp.log((2.0 * number + 1.0) / (2.0 * number)), 0.0)
    start = 0.5 * jnp.sum(terms, axis=1, keepdims=True) - 0.5 * math.log(2.0)
    starts = [start + wave * lat_ref[1:2, c * 128 : (c + 1) * 128] for c in range(2)]
    inside = [lat_ref[2:3, c * 128 : (c + 1) * 128] for c in range(2)]

    def coefficient(up, w):
        return jnp.sqrt((4.0 * (w + up) * (w + up) - 1.0) / (up * (2.0 * w + up)))

    for c in range(3):
        up = (iota((16, 128), 1) + (c * 128 + 1)).astype(F32)
        coefs[0, c] = coefficient(up, wave)
        coefs[1, c] = coefs[0, c] / coefficient(jnp.maximum(up - 1.0, 1.0), wave)

    def block(b, carry):
        current, previous, logs = (list(x) for x in carry)
        factor = [jnp.exp(starts[c] + logs[c]) * inside[c] for c in range(2)]
        shift = lax.rem(128 - 16 * lax.rem(b, 8), 128)
        coef, ratio = (pltpu.roll(coefs[n, b // 8], shift, 1) for n in range(2))
        for i in range(16):
            row = (i % 2) * HK + b * 8 + i // 2
            up, down = (jnp.broadcast_to(x[:, i : i + 1], (16, 128)) for x in (coef, ratio))
            for c in range(2):
                scratch[c, pl.ds(row, 16, stride=APART), :] = current[c] * factor[c]
                following = (up * cosines[c]) * current[c] - down * previous[c]
                previous[c] = current[c]
                current[c] = following
        for c in range(2):
            biggest = jnp.maximum(jnp.abs(current[c]), jnp.abs(previous[c]))
            shrink = 1.0 / biggest
            current[c] = current[c] * shrink
            previous[c] = previous[c] * shrink
            logs[c] = logs[c] + jnp.log(biggest)
        return tuple(current), tuple(previous), tuple(logs)

    ones = jnp.ones((16, 128), F32)
    zeros = jnp.zeros((16, 128), F32)
    part_way = lax.fori_loop(0, 3, block, ((ones, ones), (zeros, zeros), (zeros, zeros)))
    between()
    lax.fori_loop(3, M // 16, block, part_way)


def first_rows(j, w, spectra_ref, scratch, table_ref, state_ref, send_ref):
    old, new = iota((2 * COLS, 2 * COLS), 0), iota((2 * COLS, 2 * COLS), 1)
    perm = (reordered(old % COLS, new % COLS) & (old // COLS == new // COLS)).astype(BF16)
    for c in range(2):
        table_ref[j, :, c * 128 : (c + 1) * 128] = scratch[c, pl.ds(j * APART, M), :].astype(BF16)
    keep, _ = keep_of(w)
    given = jnp.concatenate(
        [spectra_ref[j, pl.ds(parity, HK, stride=2), :] for parity in range(2)], axis=0
    )
    moved = dot(split(given), perm)
    high = moved[:, :COLS] * keep
    state_ref[j] = high + moved[:, COLS:] * keep
    legendre_rows(j, table_ref, high.astype(BF16), send_ref)


def updated(j, w, table_ref, state_ref, rows_ref, mix_ref, speed):
    sides = []
    for order in (lambda d: d, lambda d: SPACE - 1 - d):
        pieces = [
            rows_ref[half, order(d), j].astype(F32) for half in range(2) for d in range(SPACE // 2)
        ]
        sides.append(jnp.concatenate(pieces, axis=0).astype(BF16))
    change = dot(table_ref[j], jnp.concatenate(sides, axis=1))
    north, south = change[:, :COLS], change[:, COLS:]
    change = jnp.concatenate([north[:HK] + south[:HK], north[HK:] - south[HK:]], axis=0)
    combined = state_ref[j] + change
    keep, degree = keep_of(w)
    stiffness = speed * (degree * (degree + 1)).astype(F32)
    damping = stiffness / (1.0 + stiffness)
    projected = dot(split(combined), mix_ref[0])
    projected = damping * (projected[:, :COLS] + projected[:, COLS:])
    returned = dot(split(projected), mix_ref[1])
    return (combined - (returned[:, :COLS] + returned[:, COLS:])) * keep


def zonal_tables(wave_ref, synth_ref, analysis_ref):
    step = 2.0 * math.pi / NLON

    def angle_of(count):
        return (count - NLON * jnp.floor(count * (1.0 / NLON))) * step

    def rows(i, _):
        at = pl.ds(pl.multiple_of(i * 64, 64), 64)
        below = pl.ds(pl.multiple_of(M + i * 64, 64), 64)
        wave = wave_ref[at, :]
        x = iota((64, 128), 1).astype(F32)
        angle = angle_of(wave * x)
        turn = angle_of(wave * jnp.full((64, 128), 128.0, F32))
        cosine, sine = jnp.cos(angle), jnp.sin(angle)
        turn_cosine, turn_sine = jnp.cos(turn), jnp.sin(turn)
        factor = jnp.where(wave == 0.0, 1.0, 2.0)
        for c in range(CHUNKS):
            width = min(128, NLON - c * 128)
            lanes = slice(c * 128, c * 128 + width)
            synth_ref[at, lanes] = (factor * cosine)[:, :width].astype(BF16)
            synth_ref[below, lanes] = (-factor * sine)[:, :width].astype(BF16)
            analysis_ref[at, lanes] = (cosine * (1.0 / NLON))[:, :width].astype(BF16)
            analysis_ref[below, lanes] = (sine * (-1.0 / NLON))[:, :width].astype(BF16)
            cosine, sine = (
                cosine * turn_cosine - sine * turn_sine,
                sine * turn_cosine + cosine * turn_sine,
            )
        return 0

    lax.fori_loop(0, M // 64, rows, 0)


def grid_half(half, weight_smem, wave_ref, rows_ref, synth_ref, analysis_ref, traj_ref, out_ref, wide, narrow):
    space = lax.axis_index("space")
    flip = space >= SPACE // 2
    first_weight = jnp.where(flip, SPACE - 1 - space, space) * LATS

    def widen(n, _):
        at = pl.ds(pl.multiple_of(n * (SLOTS * PART), SLOTS * PART), SLOTS * PART)
        wide[at, :] = rows_ref[n].astype(F32).reshape(SLOTS * PART, COLS)
        return 0

    lax.fori_loop(0, SPACE, widen, 0)
    wave = wave_ref[...]
    low = iota((M, COLS), 1) < ROWS

    def group(g, _):
        values_in, slopes_in = [], []
        for pair in range(GROUP // 2):
            t = g * GROUP + 2 * pair
            one = wide[pl.ds(t, M, stride=PART), :]
            two = wide[pl.ds(t + 1, M, stride=PART), :]
            real = jnp.where(low, one, pltpu.roll(two, ROWS, 1))
            imag = jnp.where(low, pltpu.roll(one, ROWS, 1), two)
            values_in.append(jnp.concatenate([real, imag], axis=0).astype(BF16))
            slopes_in.append(jnp.concatenate([-wave * imag, wave * real], axis=0).astype(BF16))
        values = dot(jnp.concatenate(values_in, axis=1), synth_ref[...], ((0,), (0,)))
        slopes = dot(jnp.concatenate(slopes_in, axis=1), synth_ref[...], ((0,), (0,)))
        pieces = []
        for q in range(GROUP):
            i = jnp.minimum(half * PART + g * GROUP + q, LATS - 1)
            t = jnp.where(flip, LATS - 1 - i, i)
            now = traj_ref[:, t].astype(F32)
            wind = jnp.concatenate([now[:, 0], now[:, 0]], axis=1)
            state = jnp.concatenate([now[:, 2], now[:, 1]], axis=1)
            v = values[q * ROWS : (q + 1) * ROWS].reshape(8, 8, NLON)
            s = slopes[q * ROWS : (q + 1) * ROWS].reshape(8, 8, NLON)
            forcing = (wind * s + state * v) * -weight_smem[first_weight + i]
            pieces.append(forcing.reshape(ROWS, NLON).astype(BF16))
        forcing = jnp.concatenate(pieces, axis=0)
        waves = dot(analysis_ref[...], forcing, ((1,), (1,)))
        for pair in range(GROUP // 2):
            t = g * GROUP + 2 * pair
            real = waves[0:M, pair * COLS : (pair + 1) * COLS]
            imag = waves[M : 2 * M, pair * COLS : (pair + 1) * COLS]
            narrow[pl.ds(t, M, stride=PART), :] = jnp.where(low, real, pltpu.roll(imag, ROWS, 1))
            narrow[pl.ds(t + 1, M, stride=PART), :] = jnp.where(low, pltpu.roll(real, ROWS, 1), imag)
        return 0

    lax.fori_loop(0, PART // GROUP, group, 0)

    def shrink(n, _):
        at = pl.ds(pl.multiple_of(n * (SLOTS * PART), SLOTS * PART), SLOTS * PART)
        out_ref[n] = narrow[at, :].reshape(SLOTS, PART, COLS).astype(BF16)
        return 0

    lax.fori_loop(0, SPACE, shrink, 0)


def remote(src, dst, send, recv, **to):
    return pltpu.make_async_remote_copy(
        src, dst, send, recv, device_id=to, device_id_type=MESH
    )


def steps_kernel(
    wave_smem, weight_smem, lat_ref, spectra_ref, modes_ref, speeds_ref, own_ref,
    out_ref,
    part, wave_ref, scratch, coefs, table_ref, state_ref, mix_ref, speed_ref, first_ref,
    traj, synth, analysis, there_0, there_1, grid_0, grid_1, back_0, back_1, second, middle, wide, narrow,
    send_sem, recv_sem, own_sem, ring_send, ring_recv, ring_own, part_send, part_recv,
):
    me = lax.axis_index("space")
    pert = lax.axis_index("pert")
    side, y = pert // 4, lax.rem(pert, 4)
    after, before = side * 4 + lax.rem(y + 1, 4), side * 4 + lax.rem(y + 3, 4)
    barrier = pltpu.get_barrier_semaphore()

    def greet(i, _):
        pl.semaphore_signal(
            barrier, inc=1, device_id={"space": lax.rem(me + i, SPACE)}, device_id_type=MESH
        )
        return 0

    lax.fori_loop(1, SPACE, greet, 0)
    partner = lax.rem(pert + 4, PERT)
    for neighbour in (after, before, partner):
        pl.semaphore_signal(barrier, inc=1, device_id={"pert": neighbour}, device_id_type=MESH)

    exchanges = ((first_ref, there_0), (grid_0, back_0), (second, there_1), (grid_1, back_1))

    def own_copy(e, chunk, half, slots):
        src, dst = exchanges[e]
        return pltpu.make_async_copy(
            src.at[half, me, slots], dst.at[half, me, slots], own_sem.at[e, chunk]
        )

    def push(e, chunk, half, slots=pl.ds(0, SLOTS)):
        src, dst = exchanges[e]

        def start(i, _):
            to = lax.rem(me + i, SPACE)
            remote(
                src.at[half, to, slots], dst.at[half, me, slots],
                send_sem.at[e, chunk], recv_sem.at[e, chunk], space=to,
            ).start()
            return 0

        lax.fori_loop(1, SPACE, start, 0)
        own_copy(e, chunk, half, slots).start()

    def everyone(e, chunk, half, slots):
        src, dst = exchanges[e]
        others = pl.ds(0, SPACE - 1)
        return remote(
            src.at[half, others, slots], dst.at[half, others, slots],
            send_sem.at[e, chunk], recv_sem.at[e, chunk], space=lax.rem(me + 1, SPACE),
        )

    def arrive(e, chunk, half, slots=pl.ds(0, SLOTS)):
        everyone(e, chunk, half, slots).wait_recv()
        own_copy(e, chunk, half, slots).wait()

    def drain(e, chunk, half, slots=pl.ds(0, SLOTS)):
        everyone(e, chunk, half, slots).wait_send()

    crossing = [
        remote(own_ref.at[step], part.at[step], part_send.at[step], part_recv.at[step], pert=partner)
        for step in range(STEPS)
    ]
    rings, locals_ = {}, {}
    for step in range(STEPS):
        for n, (block, group) in enumerate(
            ((own_ref.at[step], side * 4), (part.at[step], (1 - side) * 4))
        ):
            here = traj.at[step, group + y]
            locals_[step, n] = pltpu.make_async_copy(block, here, ring_own.at[step, n])
            for way, to in enumerate((after, before)):
                at = 2 * n + way
                rings[step, at] = remote(
                    block, here, ring_send.at[step, at], ring_recv.at[step, at], pert=to
                )

    def send_round(step, n):
        locals_[step, n].start()
        for way in range(2):
            rings[step, 2 * n + way].start()

    def between():
        pl.semaphore_wait(barrier, SPACE + 2)
        for step in range(STEPS):
            crossing[step].start()
        for step in range(STEPS):
            send_round(step, 0)

    recurrence(wave_smem, lat_ref, scratch, coefs, between)
    base = me * SLOTS
    few = SLOTS // 2
    early, late = pl.ds(0, few), pl.ds(few, few)
    for j in range(SLOTS):
        first_rows(j, wave_smem[base + j], spectra_ref, scratch, table_ref, state_ref, first_ref)
        if j == few - 1:
            push(0, 0, 0, early)
    push(0, 2, 0, late)
    push(0, 1, 1, early)
    push(0, 3, 1, late)

    def wave_row(i, _):
        wave_ref[pl.ds(i, 1), :] = jnp.full((1, COLS), wave_smem[i], jnp.int32).astype(F32)
        return 0

    lax.fori_loop(0, M, wave_row, 0)
    crossing[0].wait_recv()
    send_round(0, 1)
    implicit_operators(modes_ref, speeds_ref, mix_ref, speed_ref)
    passed = []

    def pass_on(step):
        cut = LATS // 2 + 1
        for n, group in enumerate((side * 4, (1 - side) * 4)):
            for way, (origin, rows, to) in enumerate((
                (group + lax.rem(y + 3, 4), pl.ds(0, cut), after),
                (group + lax.rem(y + 1, 4), pl.ds(cut, LATS - cut), before),
            )):
                rings[step, 2 * n + way].wait_recv()
                piece = traj.at[step, origin, rows]
                at = 4 + 2 * n + way
                passed.append(
                    remote(piece, piece, ring_send.at[step, at], ring_recv.at[step, at], pert=to)
                )
                passed[-1].start()

    zonal_tables(wave_ref, synth, analysis)
    crossing[1].wait_recv()
    send_round(1, 1)
    pass_on(0)
    speed = speed_ref[0:1, :]

    new, old = iota((2 * COLS, COLS), 0), iota((2 * COLS, COLS), 1)
    perm = reordered(old, new % COLS).astype(BF16)

    def slot(step, j):
        w = wave_smem[base + j]
        if step == 0:
            result = updated(j, w, table_ref, state_ref, back_0, mix_ref, speed)
            middle[j] = result
            legendre_rows(j, table_ref, result.astype(BF16), second)
        else:
            result = updated(j, w, table_ref, middle, back_1, mix_ref, speed)
            result = dot(split(result), perm)
            for parity in range(2):
                out_ref[j, pl.ds(parity, HK, stride=2), :] = result[parity * HK : (parity + 1) * HK]

    cuts = (few, 7)
    for step in range(STEPS):
        rows, out = (there_0, grid_0) if step == 0 else (there_1, grid_1)
        back = 2 * step + 1
        cut = cuts[step]
        for half in range(2):
            arrive(2 * step, half, half, early)
            arrive(2 * step, 2 + half, half, late)
            if half == 0:
                for c in passed[4 * step :]:
                    c.wait_recv()
                for n in range(2):
                    locals_[step, n].wait()
            grid_half(
                half, weight_smem, wave_ref, rows.at[half], synth, analysis, traj.at[step], out.at[half], wide, narrow
            )
            if half == 0:
                push(back, 0, 0)
            else:
                push(back, 1, 1, pl.ds(0, cut))
                push(back, 2, 1, pl.ds(cut, SLOTS - cut))
        if step == 0:
            pass_on(1)
        arrive(back, 0, 0)
        arrive(back, 1, 1, pl.ds(0, cut))
        for j in range(cut):
            slot(step, j)
        if step == 0:
            push(2, 0, 0, early)
        arrive(back, 2, 1, pl.ds(cut, SLOTS - cut))
        for j in range(cut, SLOTS):
            slot(step, j)
        if step == 0:
            push(2, 2, 0, late)
            push(2, 1, 1, early)
            push(2, 3, 1, late)
    for e in (0, 2):
        for half in range(2):
            drain(e, half, half, early)
            drain(e, 2 + half, half, late)
    for e, cut in ((1, cuts[0]), (3, cuts[1])):
        drain(e, 0, 0)
        drain(e, 1, 1, pl.ds(0, cut))
        drain(e, 2, 1, pl.ds(cut, SLOTS - cut))
    for c in list(rings.values()) + passed + crossing:
        c.wait_send()


VMEM = pl.BlockSpec(memory_space=pltpu.VMEM)
SMEM = pl.BlockSpec(memory_space=pltpu.SMEM)
ANY = pl.BlockSpec(memory_space=pl.ANY)


def shards(spectra, wave_order, traj_wind, traj_state, vertical_modes, mode_speeds):
    lat_rows, weight = northern()
    fields = jnp.concatenate([traj_wind[:, None], traj_state], axis=1)
    fields = jnp.transpose(fields, (0, 3, 1, 2, 4))
    rows_shape = (2, SPACE, SLOTS, PART, COLS)
    return pl.pallas_call(
        steps_kernel,
        out_shape=jax.ShapeDtypeStruct((SLOTS, M, COLS), F32),
        in_specs=[SMEM] * 2 + [VMEM] * 4 + [ANY],
        out_specs=VMEM,
        scratch_shapes=[
            pltpu.VMEM(fields.shape, BF16),
            pltpu.VMEM((M, COLS), F32),
            pltpu.VMEM((2, 16 * APART, 128), F32),
            pltpu.VMEM((2, 3, 16, 128), F32),
            pltpu.VMEM((SLOTS, M, HALF), BF16),
            pltpu.VMEM((SLOTS, M, COLS), F32),
            pltpu.VMEM((2, 2 * COLS, 2 * COLS), BF16),
            pltpu.VMEM((8, COLS), F32),
            pltpu.VMEM(rows_shape, BF16),
            pltpu.VMEM((STEPS, PERT, LATS, 3, 4, NLON), BF16),
            pltpu.VMEM((2 * M, NLON), BF16),
            pltpu.VMEM((2 * M, NLON), BF16),
        ]
        + [pltpu.VMEM(rows_shape, BF16)] * 7
        + [pltpu.VMEM((SLOTS, M, COLS), F32)]
        + [pltpu.VMEM((M * PART, COLS), F32)] * 2
        + [pltpu.SemaphoreType.DMA((4, 4))] * 3
        + [pltpu.SemaphoreType.DMA((STEPS, 8))] * 2
        + [pltpu.SemaphoreType.DMA((STEPS, 2))]
        + [pltpu.SemaphoreType.DMA((STEPS,))] * 2,
        compiler_params=pltpu.CompilerParams(
            collective_id=1, has_side_effects=True, vmem_limit_bytes=60 * 2**20
        ),
        name="steps",
    )(
        wave_order, jnp.asarray(weight), jnp.asarray(lat_rows), spectra,
        vertical_modes, mode_speeds[None], fields,
    )


def solution(mesh):
    placed = (
        P("space", None, "pert"),
        P(),
        P(None, "pert", "space", None),
        P(None, None, "pert", "space", None),
        P(),
        P(),
    )
    return jax.shard_map(
        shards, mesh=mesh, in_specs=placed, out_specs=P("space", None, "pert"), check_vma=False
    )
```

```python
import math

import jax
import jax.numpy as jnp
import numpy as np
from jax import lax
from jax.experimental import pallas as pl
from jax.experimental.pallas import tpu as pltpu
from jax.sharding import PartitionSpec as P

NLAT = 480
NLON = 960
M = 320
VARS = 2
LEV = 32
STEPS = 2
PERT = 8
SPACE = 32
SLOTS = M // SPACE
LATS = NLAT // SPACE
PAD = 16
HALF = (SPACE // 2) * PAD
COLS = 128
ROWS = COLS // 2
HK = M // 2
APART = M + 8
PART = PAD // 2
CHUNKS = 8
GROUP = 4
F32 = jnp.float32
BF16 = jnp.bfloat16
MESH = pl.DeviceIdType.MESH
HIGHEST = lax.Precision.HIGHEST


def dot(a, b, dims=((1,), (0,)), precision=None):
    return lax.dot_general(
        a, b, (dims, ((), ())), preferred_element_type=F32, precision=precision
    )


def iota(shape, axis):
    return lax.broadcasted_iota(jnp.int32, shape, axis)


def level_of(new):
    return new % ROWS // 8 * 4 + new % 4


def group_of(new):
    return new // ROWS * 2 + new % 8 // 4


def reordered(old, new):
    return old == new % 8 // 4 * 64 + level_of(new) * 2 + new // ROWS


def split(x):
    high = x.astype(BF16)
    return jnp.concatenate([high, (x - high.astype(F32)).astype(BF16)], axis=1)


def northern():
    place = np.arange(HALF)
    row = place // COLS * PART + place % PART
    inside = row < LATS
    lat = np.minimum(place % COLS // PART * LATS + row, NLAT // 2 - 1)
    angle = (lat + 0.5) * (math.pi / NLAT)
    rows = np.stack([np.cos(angle), np.log(np.sin(angle)), inside.astype(np.float64)])
    weight = np.sin((np.arange(NLAT // 2) + 0.5) * (math.pi / NLAT)) * (math.pi / NLAT)
    return rows.astype(np.float32), weight.astype(np.float32)


def keep_of(w):
    row = iota((M, COLS), 0)
    degree = jnp.where(row < HK, 2 * row, 2 * row - (M - 1)) + w
    keep = (degree <= M - 1) & jnp.logical_not((iota((M, COLS), 1) >= ROWS) & (w == 0))
    return keep.astype(F32), degree


def legendre_rows(j, table_ref, state, send_ref):
    even, odd = state[:HK], state[HK:]
    both = jnp.concatenate(
        [jnp.concatenate([even, even], axis=1), jnp.concatenate([odd, -odd], axis=1)], axis=0
    )
    rows = dot(table_ref[j], both, ((0,), (0,)))
    for half in range(2):
        for d in range(SPACE // 2):
            at = half * COLS + d * PART
            send_ref[half, d, j] = rows[at : at + PART, :COLS].astype(BF16)
            send_ref[half, SPACE - 1 - d, j] = rows[at : at + PART, COLS:].astype(BF16)


def implicit_operators(modes_ref, speeds_ref, mix_ref, speed_ref):
    lev = iota((LEV, COLS), 0)
    onehot = (level_of(iota((LEV, COLS), 1)) == lev).astype(F32)
    same = (group_of(iota((COLS, COLS), 0)) == group_of(iota((COLS, COLS), 1))).astype(F32)
    for way in range(2):
        spread = dot(onehot, modes_ref[...], ((0,), (1 - way,)), HIGHEST)
        mix = dot(spread, onehot, precision=HIGHEST) * same
        high = mix.astype(BF16)
        low = (mix - high.astype(F32)).astype(BF16)
        mix_ref[way, :COLS, :COLS] = high
        mix_ref[way, :COLS, COLS:] = low
        mix_ref[way, COLS:, :COLS] = high
        mix_ref[way, COLS:, COLS:] = jnp.zeros_like(low)
    speed_ref[...] = dot(jnp.broadcast_to(speeds_ref[...], (8, LEV)), onehot, precision=HIGHEST)


def recurrence(wave_smem, lat_ref, scratch, coefs, between):
    base = lax.axis_index("space") * SLOTS
    row16 = iota((16, 128), 0)
    wave = jnp.zeros((16, 128), jnp.int32)
    for j in range(SLOTS):
        wave = jnp.where(row16 == j, wave_smem[base + j], wave)
    wave = wave.astype(F32)
    cosines = [lat_ref[0:1, c * 128 : (c + 1) * 128] for c in range(2)]
    number = (iota((16, 384), 1) + 1).astype(F32)
    terms = jnp.where(number <= wave[:, 0:1], jnp.log((2.0 * number + 1.0) / (2.0 * number)), 0.0)
    start = 0.5 * jnp.sum(terms, axis=1, keepdims=True) - 0.5 * math.log(2.0)
    starts = [start + wave * lat_ref[1:2, c * 128 : (c + 1) * 128] for c in range(2)]
    inside = [lat_ref[2:3, c * 128 : (c + 1) * 128] for c in range(2)]

    def coefficient(up, w):
        return jnp.sqrt((4.0 * (w + up) * (w + up) - 1.0) / (up * (2.0 * w + up)))

    for c in range(3):
        up = (iota((16, 128), 1) + (c * 128 + 1)).astype(F32)
        coefs[0, c] = coefficient(up, wave)
        coefs[1, c] = coefs[0, c] / coefficient(jnp.maximum(up - 1.0, 1.0), wave)

    def block(b, carry):
        current, previous, logs = (list(x) for x in carry)
        factor = [jnp.exp(starts[c] + logs[c]) * inside[c] for c in range(2)]
        shift = lax.rem(128 - 16 * lax.rem(b, 8), 128)
        coef, ratio = (pltpu.roll(coefs[n, b // 8], shift, 1) for n in range(2))
        for i in range(16):
            row = (i % 2) * HK + b * 8 + i // 2
            up, down = (jnp.broadcast_to(x[:, i : i + 1], (16, 128)) for x in (coef, ratio))
            for c in range(2):
                scratch[c, pl.ds(row, 16, stride=APART), :] = current[c] * factor[c]
                following = (up * cosines[c]) * current[c] - down * previous[c]
                previous[c] = current[c]
                current[c] = following
        for c in range(2):
            biggest = jnp.maximum(jnp.abs(current[c]), jnp.abs(previous[c]))
            shrink = 1.0 / biggest
            current[c] = current[c] * shrink
            previous[c] = previous[c] * shrink
            logs[c] = logs[c] + jnp.log(biggest)
        return tuple(current), tuple(previous), tuple(logs)

    ones = jnp.ones((16, 128), F32)
    zeros = jnp.zeros((16, 128), F32)
    part_way = lax.fori_loop(0, 3, block, ((ones, ones), (zeros, zeros), (zeros, zeros)))
    between()
    lax.fori_loop(3, M // 16, block, part_way)


def first_rows(j, w, spectra_ref, scratch, table_ref, state_ref, send_ref):
    old, new = iota((2 * COLS, 2 * COLS), 0), iota((2 * COLS, 2 * COLS), 1)
    perm = (reordered(old % COLS, new % COLS) & (old // COLS == new // COLS)).astype(BF16)
    for c in range(2):
        table_ref[j, :, c * 128 : (c + 1) * 128] = scratch[c, pl.ds(j * APART, M), :].astype(BF16)
    keep, _ = keep_of(w)
    given = jnp.concatenate(
        [spectra_ref[j, pl.ds(parity, HK, stride=2), :] for parity in range(2)], axis=0
    )
    moved = dot(split(given), perm)
    high = moved[:, :COLS] * keep
    state_ref[j] = high + moved[:, COLS:] * keep
    legendre_rows(j, table_ref, high.astype(BF16), send_ref)


def updated(j, w, table_ref, state_ref, rows_ref, mix_ref, speed):
    sides = []
    for order in (lambda d: d, lambda d: SPACE - 1 - d):
        pieces = [
            rows_ref[half, order(d), j].astype(F32) for half in range(2) for d in range(SPACE // 2)
        ]
        sides.append(jnp.concatenate(pieces, axis=0).astype(BF16))
    change = dot(table_ref[j], jnp.concatenate(sides, axis=1))
    north, south = change[:, :COLS], change[:, COLS:]
    change = jnp.concatenate([north[:HK] + south[:HK], north[HK:] - south[HK:]], axis=0)
    combined = state_ref[j] + change
    keep, degree = keep_of(w)
    stiffness = speed * (degree * (degree + 1)).astype(F32)
    damping = stiffness / (1.0 + stiffness)
    projected = dot(split(combined), mix_ref[0])
    projected = damping * (projected[:, :COLS] + projected[:, COLS:])
    returned = dot(split(projected), mix_ref[1])
    return (combined - (returned[:, :COLS] + returned[:, COLS:])) * keep


def zonal_tables(wave_ref, synth_ref, analysis_ref):
    step = 2.0 * math.pi / NLON

    def angle_of(count):
        return (count - NLON * jnp.floor(count * (1.0 / NLON))) * step

    def rows(i, _):
        at = pl.ds(pl.multiple_of(i * 64, 64), 64)
        below = pl.ds(pl.multiple_of(M + i * 64, 64), 64)
        wave = wave_ref[at, :]
        x = iota((64, 128), 1).astype(F32)
        angle = angle_of(wave * x)
        turn = angle_of(wave * jnp.full((64, 128), 128.0, F32))
        cosine, sine = jnp.cos(angle), jnp.sin(angle)
        turn_cosine, turn_sine = jnp.cos(turn), jnp.sin(turn)
        factor = jnp.where(wave == 0.0, 1.0, 2.0)
        for c in range(CHUNKS):
            width = min(128, NLON - c * 128)
            lanes = slice(c * 128, c * 128 + width)
            synth_ref[at, lanes] = (factor * cosine)[:, :width].astype(BF16)
            synth_ref[below, lanes] = (-factor * sine)[:, :width].astype(BF16)
            analysis_ref[at, lanes] = (cosine * (1.0 / NLON))[:, :width].astype(BF16)
            analysis_ref[below, lanes] = (sine * (-1.0 / NLON))[:, :width].astype(BF16)
            cosine, sine = (
                cosine * turn_cosine - sine * turn_sine,
                sine * turn_cosine + cosine * turn_sine,
            )
        return 0

    lax.fori_loop(0, M // 64, rows, 0)


def grid_half(half, weight_smem, wave_ref, rows_ref, synth_ref, analysis_ref, traj_ref, out_ref, wide, narrow):
    space = lax.axis_index("space")
    flip = space >= SPACE // 2
    first_weight = jnp.where(flip, SPACE - 1 - space, space) * LATS

    def widen(n, _):
        at = pl.ds(pl.multiple_of(n * (SLOTS * PART), SLOTS * PART), SLOTS * PART)
        wide[at, :] = rows_ref[n].astype(F32).reshape(SLOTS * PART, COLS)
        return 0

    lax.fori_loop(0, SPACE, widen, 0)
    wave = wave_ref[...]
    low = iota((M, COLS), 1) < ROWS

    def group(g, _):
        values_in, slopes_in = [], []
        for pair in range(GROUP // 2):
            t = g * GROUP + 2 * pair
            one = wide[pl.ds(t, M, stride=PART), :]
            two = wide[pl.ds(t + 1, M, stride=PART), :]
            real = jnp.where(low, one, pltpu.roll(two, ROWS, 1))
            imag = jnp.where(low, pltpu.roll(one, ROWS, 1), two)
            values_in.append(jnp.concatenate([real, imag], axis=0).astype(BF16))
            slopes_in.append(jnp.concatenate([-wave * imag, wave * real], axis=0).astype(BF16))
        values = dot(jnp.concatenate(values_in, axis=1), synth_ref[...], ((0,), (0,)))
        slopes = dot(jnp.concatenate(slopes_in, axis=1), synth_ref[...], ((0,), (0,)))
        pieces = []
        for q in range(GROUP):
            i = jnp.minimum(half * PART + g * GROUP + q, LATS - 1)
            t = jnp.where(flip, LATS - 1 - i, i)
            now = traj_ref[:, t].astype(F32)
            wind = jnp.concatenate([now[:, 0], now[:, 0]], axis=1)
            state = jnp.concatenate([now[:, 2], now[:, 1]], axis=1)
            v = values[q * ROWS : (q + 1) * ROWS].reshape(8, 8, NLON)
            s = slopes[q * ROWS : (q + 1) * ROWS].reshape(8, 8, NLON)
            forcing = (wind * s + state * v) * -weight_smem[first_weight + i]
            pieces.append(forcing.reshape(ROWS, NLON).astype(BF16))
        forcing = jnp.concatenate(pieces, axis=0)
        waves = dot(analysis_ref[...], forcing, ((1,), (1,)))
        for pair in range(GROUP // 2):
            t = g * GROUP + 2 * pair
            real = waves[0:M, pair * COLS : (pair + 1) * COLS]
            imag = waves[M : 2 * M, pair * COLS : (pair + 1) * COLS]
            narrow[pl.ds(t, M, stride=PART), :] = jnp.where(low, real, pltpu.roll(imag, ROWS, 1))
            narrow[pl.ds(t + 1, M, stride=PART), :] = jnp.where(low, pltpu.roll(real, ROWS, 1), imag)
        return 0

    lax.fori_loop(0, PART // GROUP, group, 0)

    def shrink(n, _):
        at = pl.ds(pl.multiple_of(n * (SLOTS * PART), SLOTS * PART), SLOTS * PART)
        out_ref[n] = narrow[at, :].reshape(SLOTS, PART, COLS).astype(BF16)
        return 0

    lax.fori_loop(0, SPACE, shrink, 0)


def remote(src, dst, send, recv, **to):
    return pltpu.make_async_remote_copy(
        src, dst, send, recv, device_id=to, device_id_type=MESH
    )


def steps_kernel(
    wave_smem, weight_smem, lat_ref, spectra_ref, modes_ref, speeds_ref, own_ref,
    out_ref,
    part, wave_ref, scratch, coefs, table_ref, state_ref, mix_ref, speed_ref, first_ref,
    traj, synth, analysis, there_0, there_1, grid_0, grid_1, back_0, back_1, second, middle, wide, narrow,
    send_sem, recv_sem, own_sem, ring_send, ring_recv, ring_own, part_send, part_recv,
):
    me = lax.axis_index("space")
    pert = lax.axis_index("pert")
    side, y = pert // 4, lax.rem(pert, 4)
    after, before = side * 4 + lax.rem(y + 1, 4), side * 4 + lax.rem(y + 3, 4)
    barrier = pltpu.get_barrier_semaphore()

    def greet(i, _):
        pl.semaphore_signal(
            barrier, inc=1, device_id={"space": lax.rem(me + i, SPACE)}, device_id_type=MESH
        )
        return 0

    lax.fori_loop(1, SPACE, greet, 0)
    partner = lax.rem(pert + 4, PERT)
    for neighbour in (after, before, partner):
        pl.semaphore_signal(barrier, inc=1, device_id={"pert": neighbour}, device_id_type=MESH)

    exchanges = ((first_ref, there_0), (grid_0, back_0), (second, there_1), (grid_1, back_1))

    def own_copy(e, chunk, half, slots):
        src, dst = exchanges[e]
        return pltpu.make_async_copy(
            src.at[half, me, slots], dst.at[half, me, slots], own_sem.at[e, chunk]
        )

    def push(e, chunk, half, slots=pl.ds(0, SLOTS)):
        src, dst = exchanges[e]

        def start(i, _):
            to = lax.rem(me + i, SPACE)
            remote(
                src.at[half, to, slots], dst.at[half, me, slots],
                send_sem.at[e, chunk], recv_sem.at[e, chunk], space=to,
            ).start()
            return 0

        lax.fori_loop(1, SPACE, start, 0)
        own_copy(e, chunk, half, slots).start()

    def everyone(e, chunk, half, slots):
        src, dst = exchanges[e]
        others = pl.ds(0, SPACE - 1)
        return remote(
            src.at[half, others, slots], dst.at[half, others, slots],
            send_sem.at[e, chunk], recv_sem.at[e, chunk], space=lax.rem(me + 1, SPACE),
        )

    def arrive(e, chunk, half, slots=pl.ds(0, SLOTS)):
        everyone(e, chunk, half, slots).wait_recv()
        own_copy(e, chunk, half, slots).wait()

    def drain(e, chunk, half, slots=pl.ds(0, SLOTS)):
        everyone(e, chunk, half, slots).wait_send()

    crossing = [
        remote(own_ref.at[step], part.at[step], part_send.at[step], part_recv.at[step], pert=partner)
        for step in range(STEPS)
    ]
    rings, locals_ = {}, {}
    for step in range(STEPS):
        for n, (block, group) in enumerate(
            ((own_ref.at[step], side * 4), (part.at[step], (1 - side) * 4))
        ):
            here = traj.at[step, group + y]
            locals_[step, n] = pltpu.make_async_copy(block, here, ring_own.at[step, n])
            for way, to in enumerate((after, before)):
                at = 2 * n + way
                rings[step, at] = remote(
                    block, here, ring_send.at[step, at], ring_recv.at[step, at], pert=to
                )

    def send_round(step, n):
        locals_[step, n].start()
        for way in range(2):
            rings[step, 2 * n + way].start()

    def between():
        pl.semaphore_wait(barrier, SPACE + 2)
        for step in range(STEPS):
            crossing[step].start()
        for step in range(STEPS):
            send_round(step, 0)

    recurrence(wave_smem, lat_ref, scratch, coefs, between)
    base = me * SLOTS
    few = SLOTS // 2
    early, late = pl.ds(0, few), pl.ds(few, few)
    for j in range(SLOTS):
        first_rows(j, wave_smem[base + j], spectra_ref, scratch, table_ref, state_ref, first_ref)
        if j == few - 1:
            push(0, 0, 0, early)
    push(0, 2, 0, late)
    push(0, 1, 1, early)
    push(0, 3, 1, late)

    def wave_row(i, _):
        wave_ref[pl.ds(i, 1), :] = jnp.full((1, COLS), wave_smem[i], jnp.int32).astype(F32)
        return 0

    lax.fori_loop(0, M, wave_row, 0)
    crossing[0].wait_recv()
    send_round(0, 1)
    implicit_operators(modes_ref, speeds_ref, mix_ref, speed_ref)
    passed = []

    def pass_on(step):
        cut = LATS // 2 + 1
        for n, group in enumerate((side * 4, (1 - side) * 4)):
            for way, (origin, rows, to) in enumerate((
                (group + lax.rem(y + 3, 4), pl.ds(0, cut), after),
                (group + lax.rem(y + 1, 4), pl.ds(cut, LATS - cut), before),
            )):
                rings[step, 2 * n + way].wait_recv()
                piece = traj.at[step, origin, rows]
                at = 4 + 2 * n + way
                passed.append(
                    remote(piece, piece, ring_send.at[step, at], ring_recv.at[step, at], pert=to)
                )
                passed[-1].start()

    zonal_tables(wave_ref, synth, analysis)
    crossing[1].wait_recv()
    send_round(1, 1)
    pass_on(0)
    speed = speed_ref[0:1, :]

    new, old = iota((2 * COLS, COLS), 0), iota((2 * COLS, COLS), 1)
    perm = reordered(old, new % COLS).astype(BF16)

    def slot(step, j):
        w = wave_smem[base + j]
        if step == 0:
            result = updated(j, w, table_ref, state_ref, back_0, mix_ref, speed)
            middle[j] = result
            legendre_rows(j, table_ref, result.astype(BF16), second)
        else:
            result = updated(j, w, table_ref, middle, back_1, mix_ref, speed)
            result = dot(split(result), perm)
            for parity in range(2):
                out_ref[j, pl.ds(parity, HK, stride=2), :] = result[parity * HK : (parity + 1) * HK]

    cuts = (few, 7)
    for step in range(STEPS):
        rows, out = (there_0, grid_0) if step == 0 else (there_1, grid_1)
        back = 2 * step + 1
        cut = cuts[step]
        for half in range(2):
            arrive(2 * step, half, half, early)
            arrive(2 * step, 2 + half, half, late)
            if half == 0:
                for c in passed[4 * step :]:
                    c.wait_recv()
                for n in range(2):
                    locals_[step, n].wait()
            grid_half(
                half, weight_smem, wave_ref, rows.at[half], synth, analysis, traj.at[step], out.at[half], wide, narrow
            )
            if half == 0:
                push(back, 0, 0)
            else:
                push(back, 1, 1, pl.ds(0, cut))
                push(back, 2, 1, pl.ds(cut, SLOTS - cut))
        if step == 0:
            pass_on(1)
        arrive(back, 0, 0)
        arrive(back, 1, 1, pl.ds(0, cut))
        for j in range(cut):
            slot(step, j)
        if step == 0:
            push(2, 0, 0, early)
        arrive(back, 2, 1, pl.ds(cut, SLOTS - cut))
        for j in range(cut, SLOTS):
            slot(step, j)
        if step == 0:
            push(2, 2, 0, late)
            push(2, 1, 1, early)
            push(2, 3, 1, late)
    for e in (0, 2):
        for half in range(2):
            drain(e, half, half, early)
            drain(e, 2 + half, half, late)
    for e, cut in ((1, cuts[0]), (3, cuts[1])):
        drain(e, 0, 0)
        drain(e, 1, 1, pl.ds(0, cut))
        drain(e, 2, 1, pl.ds(cut, SLOTS - cut))
    for c in list(rings.values()) + passed + crossing:
        c.wait_send()


VMEM = pl.BlockSpec(memory_space=pltpu.VMEM)
SMEM = pl.BlockSpec(memory_space=pltpu.SMEM)
ANY = pl.BlockSpec(memory_space=pl.ANY)


def shards(spectra, wave_order, traj_wind, traj_state, vertical_modes, mode_speeds):
    lat_rows, weight = northern()
    fields = jnp.concatenate([traj_wind[:, None], traj_state], axis=1)
    fields = jnp.transpose(fields, (0, 3, 1, 2, 4))
    rows_shape = (2, SPACE, SLOTS, PART, COLS)
    return pl.pallas_call(
        steps_kernel,
        out_shape=jax.ShapeDtypeStruct((SLOTS, M, COLS), F32),
        in_specs=[SMEM] * 2 + [VMEM] * 4 + [ANY],
        out_specs=VMEM,
        scratch_shapes=[
            pltpu.VMEM(fields.shape, BF16),
            pltpu.VMEM((M, COLS), F32),
            pltpu.VMEM((2, 16 * APART, 128), F32),
            pltpu.VMEM((2, 3, 16, 128), F32),
            pltpu.VMEM((SLOTS, M, HALF), BF16),
            pltpu.VMEM((SLOTS, M, COLS), F32),
            pltpu.VMEM((2, 2 * COLS, 2 * COLS), BF16),
            pltpu.VMEM((8, COLS), F32),
            pltpu.VMEM(rows_shape, BF16),
            pltpu.VMEM((STEPS, PERT, LATS, 3, 4, NLON), BF16),
            pltpu.VMEM((2 * M, NLON), BF16),
            pltpu.VMEM((2 * M, NLON), BF16),
        ]
        + [pltpu.VMEM(rows_shape, BF16)] * 7
        + [pltpu.VMEM((SLOTS, M, COLS), F32)]
        + [pltpu.VMEM((M * PART, COLS), F32)] * 2
        + [pltpu.SemaphoreType.DMA((4, 4))] * 3
        + [pltpu.SemaphoreType.DMA((STEPS, 8))] * 2
        + [pltpu.SemaphoreType.DMA((STEPS, 2))]
        + [pltpu.SemaphoreType.DMA((STEPS,))] * 2,
        compiler_params=pltpu.CompilerParams(
            collective_id=1, has_side_effects=True, vmem_limit_bytes=46 * 2**20
        ),
        name="steps",
    )(
        wave_order, jnp.asarray(weight), jnp.asarray(lat_rows), spectra,
        vertical_modes, mode_speeds[None], fields,
    )


def solution(mesh):
    placed = (
        P("space", None, "pert"),
        P(),
        P(None, "pert", "space", None),
        P(None, None, "pert", "space", None),
        P(),
        P(),
    )
    return jax.shard_map(
        shards, mesh=mesh, in_specs=placed, out_specs=P("space", None, "pert"), check_vma=False
    )
```

```python
import math

import jax
import jax.numpy as jnp
import numpy as np
from jax import lax
from jax.experimental import pallas as pl
from jax.experimental.pallas import tpu as pltpu
from jax.sharding import PartitionSpec as P

NLAT = 480
NLON = 960
M = 320
VARS = 2
LEV = 32
STEPS = 2
PERT = 8
SPACE = 32
SLOTS = M // SPACE
LATS = NLAT // SPACE
PAD = 16
HALF = (SPACE // 2) * PAD
COLS = 128
ROWS = COLS // 2
HK = M // 2
APART = M + 8
PART = PAD // 2
CHUNKS = 8
GROUP = 4
F32 = jnp.float32
BF16 = jnp.bfloat16
MESH = pl.DeviceIdType.MESH
HIGHEST = lax.Precision.HIGHEST


def dot(a, b, dims=((1,), (0,)), precision=None):
    return lax.dot_general(
        a, b, (dims, ((), ())), preferred_element_type=F32, precision=precision
    )


def iota(shape, axis):
    return lax.broadcasted_iota(jnp.int32, shape, axis)


def level_of(new):
    return new % ROWS // 8 * 4 + new % 4


def group_of(new):
    return new // ROWS * 2 + new % 8 // 4


def reordered(old, new):
    return old == new % 8 // 4 * 64 + level_of(new) * 2 + new // ROWS


def split(x):
    high = x.astype(BF16)
    return jnp.concatenate([high, (x - high.astype(F32)).astype(BF16)], axis=1)


def northern():
    place = np.arange(HALF)
    row = place // COLS * PART + place % PART
    inside = row < LATS
    lat = np.minimum(place % COLS // PART * LATS + row, NLAT // 2 - 1)
    angle = (lat + 0.5) * (math.pi / NLAT)
    rows = np.stack([np.cos(angle), np.log(np.sin(angle)), inside.astype(np.float64)])
    weight = np.sin((np.arange(NLAT // 2) + 0.5) * (math.pi / NLAT)) * (math.pi / NLAT)
    return rows.astype(np.float32), weight.astype(np.float32)


def keep_of(w):
    row = iota((M, COLS), 0)
    degree = jnp.where(row < HK, 2 * row, 2 * row - (M - 1)) + w
    keep = (degree <= M - 1) & jnp.logical_not((iota((M, COLS), 1) >= ROWS) & (w == 0))
    return keep.astype(F32), degree


def legendre_rows(j, table_ref, state, send_ref):
    even, odd = state[:HK], state[HK:]
    both = jnp.concatenate(
        [jnp.concatenate([even, even], axis=1), jnp.concatenate([odd, -odd], axis=1)], axis=0
    )
    rows = dot(table_ref[j], both, ((0,), (0,)))
    for half in range(2):
        for d in range(SPACE // 2):
            at = half * COLS + d * PART
            send_ref[half, d, j] = rows[at : at + PART, :COLS].astype(BF16)
            send_ref[half, SPACE - 1 - d, j] = rows[at : at + PART, COLS:].astype(BF16)


def implicit_operators(modes_ref, speeds_ref, mix_ref, speed_ref):
    lev = iota((LEV, COLS), 0)
    onehot = (level_of(iota((LEV, COLS), 1)) == lev).astype(F32)
    same = (group_of(iota((COLS, COLS), 0)) == group_of(iota((COLS, COLS), 1))).astype(F32)
    for way in range(2):
        spread = dot(onehot, modes_ref[...], ((0,), (1 - way,)), HIGHEST)
        mix = dot(spread, onehot, precision=HIGHEST) * same
        high = mix.astype(BF16)
        low = (mix - high.astype(F32)).astype(BF16)
        mix_ref[way, :COLS, :COLS] = high
        mix_ref[way, :COLS, COLS:] = low
        mix_ref[way, COLS:, :COLS] = high
        mix_ref[way, COLS:, COLS:] = jnp.zeros_like(low)
    speed_ref[...] = dot(jnp.broadcast_to(speeds_ref[...], (8, LEV)), onehot, precision=HIGHEST)


def recurrence(wave_smem, lat_ref, scratch, coefs, between):
    base = lax.axis_index("space") * SLOTS
    row16 = iota((16, 128), 0)
    wave = jnp.zeros((16, 128), jnp.int32)
    for j in range(SLOTS):
        wave = jnp.where(row16 == j, wave_smem[base + j], wave)
    wave = wave.astype(F32)
    cosines = [lat_ref[0:1, c * 128 : (c + 1) * 128] for c in range(2)]
    number = (iota((16, 384), 1) + 1).astype(F32)
    terms = jnp.where(number <= wave[:, 0:1], jnp.log((2.0 * number + 1.0) / (2.0 * number)), 0.0)
    start = 0.5 * jnp.sum(terms, axis=1, keepdims=True) - 0.5 * math.log(2.0)
    starts = [start + wave * lat_ref[1:2, c * 128 : (c + 1) * 128] for c in range(2)]
    inside = [lat_ref[2:3, c * 128 : (c + 1) * 128] for c in range(2)]

    def coefficient(up, w):
        return jnp.sqrt((4.0 * (w + up) * (w + up) - 1.0) / (up * (2.0 * w + up)))

    for c in range(3):
        up = (iota((16, 128), 1) + (c * 128 + 1)).astype(F32)
        coefs[0, c] = coefficient(up, wave)
        coefs[1, c] = coefs[0, c] / coefficient(jnp.maximum(up - 1.0, 1.0), wave)

    def block(b, carry):
        current, previous, logs = (list(x) for x in carry)
        factor = [jnp.exp(starts[c] + logs[c]) * inside[c] for c in range(2)]
        shift = lax.rem(128 - 16 * lax.rem(b, 8), 128)
        coef, ratio = (pltpu.roll(coefs[n, b // 8], shift, 1) for n in range(2))
        for i in range(16):
            row = (i % 2) * HK + b * 8 + i // 2
            up, down = (jnp.broadcast_to(x[:, i : i + 1], (16, 128)) for x in (coef, ratio))
            for c in range(2):
                scratch[c, pl.ds(row, 16, stride=APART), :] = current[c] * factor[c]
                following = (up * cosines[c]) * current[c] - down * previous[c]
                previous[c] = current[c]
                current[c] = following
        for c in range(2):
            biggest = jnp.maximum(jnp.abs(current[c]), jnp.abs(previous[c]))
            shrink = 1.0 / biggest
            current[c] = current[c] * shrink
            previous[c] = previous[c] * shrink
            logs[c] = logs[c] + jnp.log(biggest)
        return tuple(current), tuple(previous), tuple(logs)

    ones = jnp.ones((16, 128), F32)
    zeros = jnp.zeros((16, 128), F32)
    part_way = lax.fori_loop(0, 1, block, ((ones, ones), (zeros, zeros), (zeros, zeros)))
    between()
    lax.fori_loop(1, M // 16, block, part_way)


def first_rows(j, w, spectra_ref, scratch, table_ref, state_ref, send_ref):
    old, new = iota((2 * COLS, 2 * COLS), 0), iota((2 * COLS, 2 * COLS), 1)
    perm = (reordered(old % COLS, new % COLS) & (old // COLS == new // COLS)).astype(BF16)
    for c in range(2):
        table_ref[j, :, c * 128 : (c + 1) * 128] = scratch[c, pl.ds(j * APART, M), :].astype(BF16)
    keep, _ = keep_of(w)
    given = jnp.concatenate(
        [spectra_ref[j, pl.ds(parity, HK, stride=2), :] for parity in range(2)], axis=0
    )
    moved = dot(split(given), perm)
    high = moved[:, :COLS] * keep
    state_ref[j] = high + moved[:, COLS:] * keep
    legendre_rows(j, table_ref, high.astype(BF16), send_ref)


def updated(j, w, table_ref, state_ref, rows_ref, mix_ref, speed):
    sides = []
    for order in (lambda d: d, lambda d: SPACE - 1 - d):
        pieces = [
            rows_ref[half, order(d), j].astype(F32) for half in range(2) for d in range(SPACE // 2)
        ]
        sides.append(jnp.concatenate(pieces, axis=0).astype(BF16))
    change = dot(table_ref[j], jnp.concatenate(sides, axis=1))
    north, south = change[:, :COLS], change[:, COLS:]
    change = jnp.concatenate([north[:HK] + south[:HK], north[HK:] - south[HK:]], axis=0)
    combined = state_ref[j] + change
    keep, degree = keep_of(w)
    stiffness = speed * (degree * (degree + 1)).astype(F32)
    damping = stiffness / (1.0 + stiffness)
    projected = dot(split(combined), mix_ref[0])
    projected = damping * (projected[:, :COLS] + projected[:, COLS:])
    returned = dot(split(projected), mix_ref[1])
    return (combined - (returned[:, :COLS] + returned[:, COLS:])) * keep


def zonal_tables(wave_ref, synth_ref, analysis_ref):
    step = 2.0 * math.pi / NLON

    def angle_of(count):
        return (count - NLON * jnp.floor(count * (1.0 / NLON))) * step

    def rows(i, _):
        at = pl.ds(pl.multiple_of(i * 64, 64), 64)
        below = pl.ds(pl.multiple_of(M + i * 64, 64), 64)
        wave = wave_ref[at, :]
        x = iota((64, 128), 1).astype(F32)
        angle = angle_of(wave * x)
        turn = angle_of(wave * jnp.full((64, 128), 128.0, F32))
        cosine, sine = jnp.cos(angle), jnp.sin(angle)
        turn_cosine, turn_sine = jnp.cos(turn), jnp.sin(turn)
        factor = jnp.where(wave == 0.0, 1.0, 2.0)
        for c in range(CHUNKS):
            width = min(128, NLON - c * 128)
            lanes = slice(c * 128, c * 128 + width)
            synth_ref[at, lanes] = (factor * cosine)[:, :width].astype(BF16)
            synth_ref[below, lanes] = (-factor * sine)[:, :width].astype(BF16)
            analysis_ref[at, lanes] = (cosine * (1.0 / NLON))[:, :width].astype(BF16)
            analysis_ref[below, lanes] = (sine * (-1.0 / NLON))[:, :width].astype(BF16)
            cosine, sine = (
                cosine * turn_cosine - sine * turn_sine,
                sine * turn_cosine + cosine * turn_sine,
            )
        return 0

    lax.fori_loop(0, M // 64, rows, 0)


def grid_half(half, weight_smem, wave_ref, rows_ref, synth_ref, analysis_ref, traj_ref, out_ref, wide, narrow):
    space = lax.axis_index("space")
    flip = space >= SPACE // 2
    first_weight = jnp.where(flip, SPACE - 1 - space, space) * LATS

    def widen(n, _):
        at = pl.ds(pl.multiple_of(n * (SLOTS * PART), SLOTS * PART), SLOTS * PART)
        wide[at, :] = rows_ref[n].astype(F32).reshape(SLOTS * PART, COLS)
        return 0

    lax.fori_loop(0, SPACE, widen, 0)
    wave = wave_ref[...]
    low = iota((M, COLS), 1) < ROWS

    def group(g, _):
        values_in, slopes_in = [], []
        for pair in range(GROUP // 2):
            t = g * GROUP + 2 * pair
            one = wide[pl.ds(t, M, stride=PART), :]
            two = wide[pl.ds(t + 1, M, stride=PART), :]
            real = jnp.where(low, one, pltpu.roll(two, ROWS, 1))
            imag = jnp.where(low, pltpu.roll(one, ROWS, 1), two)
            values_in.append(jnp.concatenate([real, imag], axis=0).astype(BF16))
            slopes_in.append(jnp.concatenate([-wave * imag, wave * real], axis=0).astype(BF16))
        values = dot(jnp.concatenate(values_in, axis=1), synth_ref[...], ((0,), (0,)))
        slopes = dot(jnp.concatenate(slopes_in, axis=1), synth_ref[...], ((0,), (0,)))
        pieces = []
        for q in range(GROUP):
            i = jnp.minimum(half * PART + g * GROUP + q, LATS - 1)
            t = jnp.where(flip, LATS - 1 - i, i)
            now = traj_ref[:, t].astype(F32)
            wind = jnp.concatenate([now[:, 0], now[:, 0]], axis=1)
            state = jnp.concatenate([now[:, 2], now[:, 1]], axis=1)
            v = values[q * ROWS : (q + 1) * ROWS].reshape(8, 8, NLON)
            s = slopes[q * ROWS : (q + 1) * ROWS].reshape(8, 8, NLON)
            forcing = (wind * s + state * v) * -weight_smem[first_weight + i]
            pieces.append(forcing.reshape(ROWS, NLON).astype(BF16))
        forcing = jnp.concatenate(pieces, axis=0)
        waves = dot(analysis_ref[...], forcing, ((1,), (1,)))
        for pair in range(GROUP // 2):
            t = g * GROUP + 2 * pair
            real = waves[0:M, pair * COLS : (pair + 1) * COLS]
            imag = waves[M : 2 * M, pair * COLS : (pair + 1) * COLS]
            narrow[pl.ds(t, M, stride=PART), :] = jnp.where(low, real, pltpu.roll(imag, ROWS, 1))
            narrow[pl.ds(t + 1, M, stride=PART), :] = jnp.where(low, pltpu.roll(real, ROWS, 1), imag)
        return 0

    lax.fori_loop(0, PART // GROUP, group, 0)

    def shrink(n, _):
        at = pl.ds(pl.multiple_of(n * (SLOTS * PART), SLOTS * PART), SLOTS * PART)
        out_ref[n] = narrow[at, :].reshape(SLOTS, PART, COLS).astype(BF16)
        return 0

    lax.fori_loop(0, SPACE, shrink, 0)


def remote(src, dst, send, recv, **to):
    return pltpu.make_async_remote_copy(
        src, dst, send, recv, device_id=to, device_id_type=MESH
    )


def steps_kernel(
    wave_smem, weight_smem, lat_ref, spectra_ref, modes_ref, speeds_ref, own_ref,
    out_ref,
    part, wave_ref, scratch, coefs, table_ref, state_ref, mix_ref, speed_ref, first_ref,
    traj, synth, analysis, there_0, there_1, grid_0, grid_1, back_0, back_1, second, middle, wide, narrow,
    send_sem, recv_sem, own_sem, ring_send, ring_recv, ring_own, part_send, part_recv,
):
    me = lax.axis_index("space")
    pert = lax.axis_index("pert")
    side, y = pert // 4, lax.rem(pert, 4)
    after, before = side * 4 + lax.rem(y + 1, 4), side * 4 + lax.rem(y + 3, 4)
    barrier = pltpu.get_barrier_semaphore()

    def greet(i, _):
        pl.semaphore_signal(
            barrier, inc=1, device_id={"space": lax.rem(me + i, SPACE)}, device_id_type=MESH
        )
        return 0

    lax.fori_loop(1, SPACE, greet, 0)
    partner = lax.rem(pert + 4, PERT)
    for neighbour in (after, before, partner):
        pl.semaphore_signal(barrier, inc=1, device_id={"pert": neighbour}, device_id_type=MESH)

    exchanges = ((first_ref, there_0), (grid_0, back_0), (second, there_1), (grid_1, back_1))

    def own_copy(e, chunk, half, slots):
        src, dst = exchanges[e]
        return pltpu.make_async_copy(
            src.at[half, me, slots], dst.at[half, me, slots], own_sem.at[e, chunk]
        )

    def push(e, chunk, half, slots=pl.ds(0, SLOTS)):
        src, dst = exchanges[e]

        def start(i, _):
            to = lax.rem(me + i, SPACE)
            remote(
                src.at[half, to, slots], dst.at[half, me, slots],
                send_sem.at[e, chunk], recv_sem.at[e, chunk], space=to,
            ).start()
            return 0

        lax.fori_loop(1, SPACE, start, 0)
        own_copy(e, chunk, half, slots).start()

    def everyone(e, chunk, half, slots):
        src, dst = exchanges[e]
        others = pl.ds(0, SPACE - 1)
        return remote(
            src.at[half, others, slots], dst.at[half, others, slots],
            send_sem.at[e, chunk], recv_sem.at[e, chunk], space=lax.rem(me + 1, SPACE),
        )

    def arrive(e, chunk, half, slots=pl.ds(0, SLOTS)):
        everyone(e, chunk, half, slots).wait_recv()
        own_copy(e, chunk, half, slots).wait()

    def drain(e, chunk, half, slots=pl.ds(0, SLOTS)):
        everyone(e, chunk, half, slots).wait_send()

    crossing = [
        remote(own_ref.at[step], part.at[step], part_send.at[step], part_recv.at[step], pert=partner)
        for step in range(STEPS)
    ]
    rings, locals_ = {}, {}
    for step in range(STEPS):
        for n, (block, group) in enumerate(
            ((own_ref.at[step], side * 4), (part.at[step], (1 - side) * 4))
        ):
            here = traj.at[step, group + y]
            locals_[step, n] = pltpu.make_async_copy(block, here, ring_own.at[step, n])
            for way, to in enumerate((after, before)):
                at = 2 * n + way
                rings[step, at] = remote(
                    block, here, ring_send.at[step, at], ring_recv.at[step, at], pert=to
                )

    def send_round(step, n):
        locals_[step, n].start()
        for way in range(2):
            rings[step, 2 * n + way].start()

    def between():
        pl.semaphore_wait(barrier, SPACE + 2)
        for step in range(STEPS):
            crossing[step].start()
        for step in range(STEPS):
            send_round(step, 0)

    recurrence(wave_smem, lat_ref, scratch, coefs, between)
    base = me * SLOTS
    few = SLOTS // 2
    early, late = pl.ds(0, few), pl.ds(few, few)
    for j in range(SLOTS):
        first_rows(j, wave_smem[base + j], spectra_ref, scratch, table_ref, state_ref, first_ref)
        if j == few - 1:
            push(0, 0, 0, early)
    push(0, 2, 0, late)
    push(0, 1, 1, early)
    push(0, 3, 1, late)

    def wave_row(i, _):
        wave_ref[pl.ds(i, 1), :] = jnp.full((1, COLS), wave_smem[i], jnp.int32).astype(F32)
        return 0

    lax.fori_loop(0, M, wave_row, 0)
    crossing[0].wait_recv()
    send_round(0, 1)
    implicit_operators(modes_ref, speeds_ref, mix_ref, speed_ref)
    passed = []

    def pass_on(step):
        cut = LATS // 2 + 1
        for n, group in enumerate((side * 4, (1 - side) * 4)):
            for way, (origin, rows, to) in enumerate((
                (group + lax.rem(y + 3, 4), pl.ds(0, cut), after),
                (group + lax.rem(y + 1, 4), pl.ds(cut, LATS - cut), before),
            )):
                rings[step, 2 * n + way].wait_recv()
                piece = traj.at[step, origin, rows]
                at = 4 + 2 * n + way
                passed.append(
                    remote(piece, piece, ring_send.at[step, at], ring_recv.at[step, at], pert=to)
                )
                passed[-1].start()

    zonal_tables(wave_ref, synth, analysis)
    crossing[1].wait_recv()
    send_round(1, 1)
    pass_on(0)
    speed = speed_ref[0:1, :]

    new, old = iota((2 * COLS, COLS), 0), iota((2 * COLS, COLS), 1)
    perm = reordered(old, new % COLS).astype(BF16)

    def slot(step, j):
        w = wave_smem[base + j]
        if step == 0:
            result = updated(j, w, table_ref, state_ref, back_0, mix_ref, speed)
            middle[j] = result
            legendre_rows(j, table_ref, result.astype(BF16), second)
        else:
            result = updated(j, w, table_ref, middle, back_1, mix_ref, speed)
            result = dot(split(result), perm)
            for parity in range(2):
                out_ref[j, pl.ds(parity, HK, stride=2), :] = result[parity * HK : (parity + 1) * HK]

    cuts = (few, 7)
    for step in range(STEPS):
        rows, out = (there_0, grid_0) if step == 0 else (there_1, grid_1)
        back = 2 * step + 1
        cut = cuts[step]
        for half in range(2):
            arrive(2 * step, half, half, early)
            arrive(2 * step, 2 + half, half, late)
            if half == 0:
                for c in passed[4 * step :]:
                    c.wait_recv()
                for n in range(2):
                    locals_[step, n].wait()
            grid_half(
                half, weight_smem, wave_ref, rows.at[half], synth, analysis, traj.at[step], out.at[half], wide, narrow
            )
            if half == 0:
                push(back, 0, 0)
            else:
                push(back, 1, 1, pl.ds(0, cut))
                push(back, 2, 1, pl.ds(cut, SLOTS - cut))
        if step == 0:
            pass_on(1)
        arrive(back, 0, 0)
        arrive(back, 1, 1, pl.ds(0, cut))
        for j in range(cut):
            slot(step, j)
        if step == 0:
            push(2, 0, 0, early)
        arrive(back, 2, 1, pl.ds(cut, SLOTS - cut))
        for j in range(cut, SLOTS):
            slot(step, j)
        if step == 0:
            push(2, 2, 0, late)
            push(2, 1, 1, early)
            push(2, 3, 1, late)
    for e in (0, 2):
        for half in range(2):
            drain(e, half, half, early)
            drain(e, 2 + half, half, late)
    for e, cut in ((1, cuts[0]), (3, cuts[1])):
        drain(e, 0, 0)
        drain(e, 1, 1, pl.ds(0, cut))
        drain(e, 2, 1, pl.ds(cut, SLOTS - cut))
    for c in list(rings.values()) + passed + crossing:
        c.wait_send()


VMEM = pl.BlockSpec(memory_space=pltpu.VMEM)
SMEM = pl.BlockSpec(memory_space=pltpu.SMEM)
ANY = pl.BlockSpec(memory_space=pl.ANY)


def shards(spectra, wave_order, traj_wind, traj_state, vertical_modes, mode_speeds):
    lat_rows, weight = northern()
    fields = jnp.concatenate([traj_wind[:, None], traj_state], axis=1)
    fields = jnp.transpose(fields, (0, 3, 1, 2, 4))
    rows_shape = (2, SPACE, SLOTS, PART, COLS)
    return pl.pallas_call(
        steps_kernel,
        out_shape=jax.ShapeDtypeStruct((SLOTS, M, COLS), F32),
        in_specs=[SMEM] * 2 + [VMEM] * 4 + [ANY],
        out_specs=VMEM,
        scratch_shapes=[
            pltpu.VMEM(fields.shape, BF16),
            pltpu.VMEM((M, COLS), F32),
            pltpu.VMEM((2, 16 * APART, 128), F32),
            pltpu.VMEM((2, 3, 16, 128), F32),
            pltpu.VMEM((SLOTS, M, HALF), BF16),
            pltpu.VMEM((SLOTS, M, COLS), F32),
            pltpu.VMEM((2, 2 * COLS, 2 * COLS), BF16),
            pltpu.VMEM((8, COLS), F32),
            pltpu.VMEM(rows_shape, BF16),
            pltpu.VMEM((STEPS, PERT, LATS, 3, 4, NLON), BF16),
            pltpu.VMEM((2 * M, NLON), BF16),
            pltpu.VMEM((2 * M, NLON), BF16),
        ]
        + [pltpu.VMEM(rows_shape, BF16)] * 7
        + [pltpu.VMEM((SLOTS, M, COLS), F32)]
        + [pltpu.VMEM((M * PART, COLS), F32)] * 2
        + [pltpu.SemaphoreType.DMA((4, 4))] * 3
        + [pltpu.SemaphoreType.DMA((STEPS, 8))] * 2
        + [pltpu.SemaphoreType.DMA((STEPS, 2))]
        + [pltpu.SemaphoreType.DMA((STEPS,))] * 2,
        compiler_params=pltpu.CompilerParams(
            collective_id=1, has_side_effects=True, vmem_limit_bytes=60 * 2**20
        ),
        name="steps",
    )(
        wave_order, jnp.asarray(weight), jnp.asarray(lat_rows), spectra,
        vertical_modes, mode_speeds[None], fields,
    )


def solution(mesh):
    placed = (
        P("space", None, "pert"),
        P(),
        P(None, "pert", "space", None),
        P(None, None, "pert", "space", None),
        P(),
        P(),
    )
    return jax.shard_map(
        shards, mesh=mesh, in_specs=placed, out_specs=P("space", None, "pert"), check_vma=False
    )
```
